768 devices in a mesh: brick: 48 (over y, z_lo), level: 16 (over x, z_hi, core).
Axes of the slice: x: 4, y: 8, z: 12 (z_hi: 2, z_lo: 6; z = z_hi * 6 + z_lo), core: 2. Of those that a mesh axis runs over, the one named last changes fastest.
Arguments:
- adjoint: float32 [5, 128, 384, 128], P(None, 'level', 'brick'), may hold values from -6 to 6
- source: float32 [5, 128, 384, 128], P(None, 'level', 'brick'), may hold values from -48 to 48
- block: bfloat16 [5, 5, 128, 384, 128], P(None, None, 'level', 'brick'), may hold values from -1 to 13
- precond: bfloat16 [5, 5, 128, 384, 128], P(None, None, 'level', 'brick'), may hold values from -0.01 to 0.14
- couple: float32 [3, 128, 384, 128], P(None, 'level', 'brick'), may hold values from 0.1 to 0.6
- solid: int32 [128, 384, 128], P('level', 'brick'), may hold values 0 or 1
- coarse_owner: int32 [16], replicated, may hold values from 0 to 15, each once
Outputs:
- smoothed: float32 [5, 128, 384, 128], P(None, 'level', 'brick')
- coarse_rhs: float32 [16, 5, 64, 192, 4], P('level', None, None, 'brick')
The draws below stay inside these ranges and needn't reach their ends.
Inputs may be any that keep to these rules, and one draw needn't show every extreme that they name: `coarse_owner`: each level index owns exactly one block.
All inputs are finite; a program needn't handle non-finite values. No bound on the sum of `solid` on one device may be relied on, other than what follows from the above.
Results may differ from the reference program's by a relative error of at most 0.0003.
Values may be sent and summed in bfloat16 or wider, within the bound.
No kernel may reach another device: no remote copies, remote signals or barrier semaphores. Data moves between devices by JAX's collectives and lax.ppermute only.
A program may use at most 32 MiB of HBM per device.

```python
import jax
import jax.numpy as jnp
from jax import lax

FIELDS = 5
SWEEPS = 4
NX = 128
NY = 384
NZ = 128
N_LEVEL = 16


def diagonal_scale(key):
    return jax.random.uniform(jax.random.fold_in(key, 11), (NX, NY, NZ), jnp.float32, 8.0, 12.0)


def draw_block(key, part):
    scale_cells = diagonal_scale(key)
    spread = jax.random.uniform(jax.random.fold_in(key, 12), (FIELDS, FIELDS, NX, NY, NZ), jnp.float32, -0.06, 0.06)
    identity = jnp.eye(FIELDS, dtype=jnp.float32)[:, :, None, None, None]
    return (scale_cells * (identity + spread)).astype(jnp.bfloat16)


def draw_precond(key, part):
    scale_cells = diagonal_scale(key)
    spread = jax.random.uniform(jax.random.fold_in(key, 13), (FIELDS, FIELDS, NX, NY, NZ), jnp.float32, -0.06, 0.06)
    identity = jnp.eye(FIELDS, dtype=jnp.float32)[:, :, None, None, None]
    return ((identity + spread) / scale_cells).astype(jnp.bfloat16)


def set_ends(values, key, smallest, high):
    shape = values.shape
    spot = [jax.random.randint(jax.random.fold_in(key, axis), (), 0, shape[axis]) for axis in range(len(shape))]
    values = values.at[tuple(spot)].set(smallest)
    longest = shape.index(max(shape))
    spot[longest] = (spot[longest] + 1) % shape[longest]
    return values.at[tuple(spot)].set(high)


def level_of(stream_key, shape, cuts, low, largest):
    def one(position, blocks):
        steps = jax.random.uniform(jax.random.fold_in(jax.random.fold_in(stream_key, 6), position), (blocks,), jnp.float32, low / len(cuts), largest / len(cuts))
        return jnp.repeat(jnp.exp(steps), shape[position] // blocks).reshape((-1,) + (1,) * (len(shape) - position - 1))

    loudness = one(*cuts[0])
    for cut in cuts[1:]:
        loudness = loudness * one(*cut)
    return loudness


def bell_draw(rng, shape, scale, limit, shards=(), kind=jnp.bfloat16):
    entries = scale * jax.random.normal(rng, shape, jnp.float32)
    if shards:
        entries = entries * level_of(rng, shape, shards, -0.22, 0.18)
    return jnp.clip(entries, -limit, limit).astype(kind)


def setup_inputs(seed: int = 0) -> dict:
    key_of = jax.random.split(jax.random.key(seed), 8)
    adjoint = bell_draw(key_of[0], (FIELDS, NX, NY, NZ), 1.0, 6.0, ((1, 16), (2, 48)), jnp.float32)
    source = bell_draw(key_of[1], (FIELDS, NX, NY, NZ), 8.0, 48.0, ((1, 16), (2, 48)), jnp.float32)
    block = draw_block(jax.random.fold_in(key_of[7], 71), 0)
    precond = draw_precond(jax.random.fold_in(key_of[7], 71), 0)
    couple = jnp.clip(0.1 + 0.5 * jax.random.uniform(key_of[4], (3, NX, NY, NZ), jnp.float32) ** level_of(key_of[4], (3, NX, NY, NZ), ((1, 16), (2, 48)), -0.2, 0.2), 0.1, 0.6)
    solid = set_ends((jax.random.randint(key_of[5], (NX, NY, NZ), 0, 8) < 1).astype(jnp.int32), jax.random.fold_in(key_of[5], 1), 0, 1)
    coarse_owner = jax.random.permutation(key_of[6], N_LEVEL).astype(jnp.int32)
    return {"adjoint": adjoint, "source": source, "block": block, "precond": precond, "couple": couple, "solid": solid, "coarse_owner": coarse_owner}


relax_factor = 0.8


def apply_operator(padded, block, couple):
    center = padded[:, 1:-1, 1:-1, :]
    fields = []
    for outer in range(FIELDS):
        total = block[0, outer].astype(jnp.float32) * center[0]
        for inner in range(1, FIELDS):
            total = total + block[inner, outer].astype(jnp.float32) * center[inner]
        fields.append(total)
    diagonal_part = jnp.stack(fields)
    across_x = padded[:, 2:, 1:-1, :] + padded[:, :-2, 1:-1, :]
    across_y = padded[:, 1:-1, 2:, :] + padded[:, 1:-1, :-2, :]
    zero_plane = jnp.zeros_like(center[..., :1])
    across_z = jnp.concatenate([center[..., 1:], zero_plane], -1) + jnp.concatenate([zero_plane, center[..., :-1]], -1)
    coupled = couple[0] * across_x + couple[1] * across_y + couple[2] * across_z
    return diagonal_part - coupled


def precondition(precond, defect):
    fields = []
    for outer in range(FIELDS):
        total = precond[outer, 0].astype(jnp.float32) * defect[0]
        for inner in range(1, FIELDS):
            total = total + precond[outer, inner].astype(jnp.float32) * defect[inner]
        fields.append(total)
    return jnp.stack(fields)


def restrict_along(field, axis, before):
    length = field.shape[axis]
    even = lax.slice_in_dim(field, 0, length, 2, axis)
    odd = lax.slice_in_dim(field, 1, length, 2, axis)
    earlier = jnp.concatenate([before, lax.slice_in_dim(odd, 0, odd.shape[axis] - 1, 1, axis)], axis)
    return 0.5 * even + 0.25 * odd + 0.25 * earlier


def zero_first(field, axis):
    return jnp.zeros_like(lax.slice_in_dim(field, 0, 1, 1, axis))


def reference(adjoint, source, block, precond, couple, solid, coarse_owner):
    keep = solid == 0
    smoothed = adjoint
    for sweep in range(SWEEPS):
        padded = jnp.pad(smoothed, ((0, 0), (1, 1), (1, 1), (0, 0)))
        defect = source - apply_operator(padded, block, couple)
        smoothed = jnp.where(keep, smoothed + relax_factor * precondition(precond, defect), 0.0)
    padded = jnp.pad(smoothed, ((0, 0), (1, 1), (1, 1), (0, 0)))
    residual = jnp.where(keep, source - apply_operator(padded, block, couple), 0.0)
    coarse_z = restrict_along(residual, 3, zero_first(residual, 3))
    coarse_y = restrict_along(coarse_z, 2, zero_first(coarse_z, 2))
    coarse = restrict_along(coarse_y, 1, zero_first(coarse_y, 1))
    pieces = coarse.reshape(FIELDS, NX // 2, NY // 2, N_LEVEL, NZ // (2 * N_LEVEL)).transpose(3, 0, 1, 2, 4)
    coarse_rhs = jnp.zeros_like(pieces).at[coarse_owner].set(pieces)
    return smoothed, coarse_rhs
```

```python
import jax
import jax.numpy as jnp
from jax import lax
from jax.sharding import PartitionSpec as P

SWEEPS = 4
relax_factor = 0.8
BOTH = ("brick", "level")


def far_pairs(count):
    return [(i, (i + 1) % count) for i in range(1, count, 2)]


def near_pairs(count):
    return [(i, i + 1) for i in range(0, count, 2)]


def split_wide(values):
    high = lax.reduce_precision(values, 8, 7)
    low = values - high
    return high.astype(jnp.bfloat16), low.astype(jnp.bfloat16)


def join_wide(high, low):
    return high.astype(jnp.float32) + low.astype(jnp.float32)


def matvec(rows, cells):
    count = cells.shape[0]
    fields = []
    for outer in range(count):
        total = rows(outer, 0) * cells[0]
        for inner in range(1, count):
            total = total + rows(outer, inner) * cells[inner]
        fields.append(total)
    return jnp.stack(fields)


def along_z(cells):
    zero = jnp.zeros_like(cells[..., :1])
    return jnp.concatenate([cells[..., 1:], zero], -1) + jnp.concatenate([zero, cells[..., :-1]], -1)


def operator(cells, neighbours, block, couple):
    diagonal = matvec(lambda outer, inner: block[inner, outer].astype(jnp.float32), cells)
    coupled = (
        couple[0] * neighbours[0] + couple[1] * neighbours[1] + couple[2] * along_z(cells)
    )
    return diagonal - coupled


def relaxed(cells, neighbours, block, precond, source, couple, keep):
    defect = source - operator(cells, neighbours, block, couple)
    step = matvec(lambda outer, inner: precond[outer, inner].astype(jnp.float32), defect)
    return jnp.where(keep, cells + relax_factor * step, 0.0)


def shards(adjoint, source, block, precond, couple, solid, coarse_owner):
    levels = lax.axis_size("level")
    bricks = lax.axis_size("brick")
    level = lax.axis_index("level")
    brick = lax.axis_index("brick")
    odd_l = level % 2 == 1
    odd_b = brick % 2 == 1
    fields = adjoint.shape[0]
    last = adjoint.shape[1] - 1
    keep = solid == 0

    f_valid = jnp.where(odd_l, level < levels - 1, level > 0)
    b_valid = jnp.where(odd_b, brick < bricks - 1, brick > 0)

    quads = [
        [b * levels + l for b in pair for l in side]
        for pair in far_pairs(bricks)
        for side in far_pairs(levels)
    ]
    a_groups = [list(pair) for pair in near_pairs(bricks)]
    n_groups = [list(pair) for pair in near_pairs(levels)]
    columns = [
        [b * levels + l for b in pair for l in range(levels)] for pair in far_pairs(bricks)
    ]

    def x_row(values, depth, above):
        low = values[..., depth, :, :]
        high = values[..., last - depth, :, :]
        return jnp.where(above, high, low)

    def y_row(values, depth, above):
        low = values[..., depth, :]
        high = values[..., last - depth, :]
        return jnp.where(above, high, low)

    edge_at = {
        "F": lambda v, d: x_row(v, d, odd_l),
        "N": lambda v, d: x_row(v, d, ~odd_l),
        "A": lambda v, d: y_row(v, d, ~odd_b),
        "B": lambda v, d: y_row(v, d, odd_b),
    }

    def facing(side, strip):
        above = {"F": odd_l, "N": ~odd_l, "A": ~odd_b, "B": odd_b}[side]
        return jnp.where(above, strip[..., last, :], strip[..., 0, :])

    def facing_back(side, strip):
        above = {"F": odd_l, "N": ~odd_l, "A": ~odd_b, "B": odd_b}[side]
        return jnp.where(above, strip[..., 0, :], strip[..., last, :])

    def state_planes(cells, side):
        both = jnp.concatenate([edge_at[side](cells, 0), edge_at[side](cells, 1)], 0)
        high, low = split_wide(both)
        return jnp.concatenate([high, low], 0)

    def fixed_planes(side):
        at = edge_at[side]
        order = (0, 1) if side in "FN" else (1, 0)
        pair = jnp.stack([couple[order[0]], couple[order[1]], couple[2]])
        wide = jnp.concatenate([at(source, 0), at(pair, 0)], 0)
        high, low = split_wide(wide)
        count = fields * fields
        return jnp.concatenate(
            [
                high,
                low,
                at(solid, 0)[None].astype(jnp.bfloat16),
                at(block, 0).reshape((count,) + high.shape[1:]),
                at(precond, 0).reshape((count,) + high.shape[1:]),
            ],
            0,
        )

    n_state = 4 * fields
    n_wide = fields + 3

    def corner_planes(corner):
        high, low = split_wide(corner)
        rows = last + 1
        return jnp.pad(jnp.stack([high, low]), ((0, 0), (0, rows - fields), (0, 0)))

    def corner_of(planes):
        return join_wide(planes[0, :fields], planes[1, :fields])

    def near_state(planes):
        return join_wide(planes[:fields], planes[2 * fields : 3 * fields])

    def deep_state(planes):
        return join_wide(planes[fields : 2 * fields], planes[3 * fields : 4 * fields])

    def exchange(cells, fixed):
        planes = {}
        for side in "FNAB":
            parts = [state_planes(cells, side)]
            if fixed is not None:
                parts.append(fixed[side])
            planes[side] = jnp.concatenate(parts, 0)
        to_even = jnp.where(odd_l, planes["F"], planes["B"])
        to_odd = jnp.where(odd_l, planes["B"], planes["F"])
        send = jnp.stack([to_odd, to_even, to_odd, to_even])
        got = lax.all_to_all(
            send, BOTH, split_axis=0, concat_axis=0, tiled=True, axis_index_groups=quads
        )
        mine = jnp.where(odd_b, got[:2], got[2:])
        other = jnp.where(odd_b, got[2:], got[:2])
        f_got = jnp.where(odd_l, mine[1], mine[0])
        b_got = jnp.where(odd_l, other[0], other[1])
        d_got = jnp.where(odd_l, other[1], other[0])
        zero = jnp.zeros((), jnp.float32)
        f_near = jnp.where(f_valid, near_state(f_got), zero)
        f_deep = jnp.where(f_valid, deep_state(f_got), zero)
        b_near = jnp.where(b_valid, near_state(b_got), zero)
        b_deep = jnp.where(b_valid, deep_state(b_got), zero)
        fb = jnp.where(f_valid & b_valid, facing_back("B", near_state(d_got)), zero)
        payload = jnp.concatenate([planes["A"], corner_planes(facing("A", f_near))], 0)
        got = lax.all_gather(payload, "brick", axis_index_groups=a_groups)
        a_got = jnp.where(odd_b, got[0], got[1])
        a_near, a_deep = near_state(a_got), deep_state(a_got)
        fa = corner_of(a_got[-2:])
        payload = jnp.concatenate(
            [
                planes["N"],
                corner_planes(facing("N", a_near)),
                corner_planes(facing("N", b_near)),
            ],
            0,
        )
        got = lax.all_gather(payload, "level", axis_index_groups=n_groups)
        n_got = jnp.where(odd_l, got[0], got[1])
        n_near, n_deep = near_state(n_got), deep_state(n_got)
        na = corner_of(n_got[-4:-2])
        nb = corner_of(n_got[-2:])

        strips = jnp.stack([f_near, n_near, a_near, b_near], 1)
        deep = jnp.stack([f_deep, n_deep, a_deep, b_deep], 1)
        low = jnp.stack(
            [
                jnp.where(odd_b, fa, fb),
                jnp.where(odd_b, na, nb),
                jnp.where(odd_l, na, fa),
                jnp.where(odd_l, nb, fb),
            ],
            1,
        )
        high = jnp.stack(
            [
                jnp.where(odd_b, fb, fa),
                jnp.where(odd_b, nb, na),
                jnp.where(odd_l, fa, na),
                jnp.where(odd_l, fb, nb),
            ],
            1,
        )
        received = {"F": f_got, "N": n_got, "A": a_got, "B": b_got}
        return strips, deep, low, high, received

    def around(strips):
        f, n, a, b = (strips[:, i] for i in range(4))
        x_low, x_high = jnp.where(odd_l, n, f), jnp.where(odd_l, f, n)
        y_low, y_high = jnp.where(odd_b, a, b), jnp.where(odd_b, b, a)
        return x_low, x_high, y_low, y_high

    def own_neighbours(cells, sides):
        x_low, x_high, y_low, y_high = sides
        tall = jnp.concatenate([x_low[:, None], cells, x_high[:, None]], 1)
        wide = jnp.concatenate([y_low[:, :, None], cells, y_high[:, :, None]], 2)
        return tall[:, 2:] + tall[:, :-2], wide[:, :, 2:] + wide[:, :, :-2]

    def inner_edges(cells):
        return jnp.stack([edge_at[side](cells, 0) for side in "FNAB"], 1)

    def strip_neighbours(cells, strips, deep, low, high):
        before = jnp.concatenate([low[:, :, None], strips[:, :, :-1]], 2)
        after = jnp.concatenate([strips[:, :, 1:], high[:, :, None]], 2)
        return deep + inner_edges(cells), before + after

    fixed = {side: fixed_planes(side) for side in "FNAB"}
    cells = adjoint
    ring = None
    for _ in range(SWEEPS // 2):
        strips, deep, low, high, received = exchange(cells, fixed if ring is None else None)
        if ring is None:
            wide = []
            masks = []
            blocks = []
            preconds = []
            for side in "FNAB":
                rest = received[side][n_state:]
                wide.append(join_wide(rest[:n_wide], rest[n_wide : 2 * n_wide]))
                open_cells = rest[2 * n_wide] == 0
                if side == "F":
                    open_cells = open_cells & f_valid
                if side == "B":
                    open_cells = open_cells & b_valid
                masks.append(open_cells)
                start = 2 * n_wide + 1
                count = fields * fields
                shape = (fields, fields) + rest.shape[1:]
                blocks.append(rest[start : start + count].reshape(shape))
                preconds.append(rest[start + count : start + 2 * count].reshape(shape))
            wide = jnp.stack(wide, 1)
            ring = {
                "source": wide[:fields],
                "couple": wide[fields:],
                "keep": jnp.stack(masks),
                "block": jnp.stack(blocks, 2),
                "precond": jnp.stack(preconds, 2),
            }
        first = relaxed(
            cells, own_neighbours(cells, around(strips)), block, precond, source, couple, keep
        )
        strips = relaxed(
            strips,
            strip_neighbours(cells, strips, deep, low, high),
            ring["block"],
            ring["precond"],
            ring["source"],
            ring["couple"],
            ring["keep"],
        )
        cells = relaxed(
            first, own_neighbours(first, around(strips)), block, precond, source, couple, keep
        )
    smoothed = cells

    nothing = jnp.zeros_like(strips)
    inside = own_neighbours(cells, around(nothing))
    residual = jnp.where(keep, source - operator(cells, inside, block, couple), 0.0)
    beyond = jnp.where(ring["keep"], ring["couple"][0] * inner_edges(cells), 0.0)
    x_low, x_high, y_low, y_high = around(beyond)

    def restrict(before, values, after, axis):
        length = values.shape[axis]
        even = lax.slice_in_dim(values, 0, length, 2, axis)
        odd = lax.slice_in_dim(values, 1, length, 2, axis)
        even = jnp.concatenate([jnp.zeros_like(before), even, after], axis)
        odd = jnp.concatenate([before, odd], axis)
        none = jnp.zeros_like(before)
        return (
            0.5 * even
            + 0.25 * jnp.concatenate([odd, none], axis)
            + 0.25 * jnp.concatenate([none, odd], axis)
        )

    along_x = restrict(x_low[:, None], residual, x_high[:, None], 1)
    blank = jnp.zeros_like(y_low[:, :1])
    y_low = restrict(blank, y_low, blank, 1)
    y_high = restrict(blank, y_high, blank, 1)
    both = restrict(y_low[:, :, None], along_x, y_high[:, :, None], 2)
    half_y = both.shape[2] - 2
    below, own, above = both[:, :, 0], both[:, :, 1:-1], both[:, :, -1]
    a_row = jnp.where(odd_b, below, above)
    b_row = jnp.where(odd_b, above, below)
    got = lax.all_gather(a_row, "brick", axis_index_groups=a_groups)
    a_got = jnp.where(odd_b, got[0], got[1])
    at_row = lax.broadcasted_iota(jnp.int32, (half_y, 1), 0)
    a_at = jnp.where(odd_b, 0, half_y - 1)
    own = own + jnp.where(at_row == a_at, a_got[:, :, None], 0.0)

    nz = adjoint.shape[3]
    zblock = nz // (2 * levels)
    slots = jnp.arange(levels, dtype=jnp.int32)
    inverse = jnp.sum(jnp.where(coarse_owner[None, :] == slots[:, None], slots[None, :], 0), axis=1)
    target = (inverse[:, None] * zblock + jnp.arange(zblock, dtype=jnp.int32)[None, :]).reshape(-1, 1)
    fine = jnp.arange(nz, dtype=jnp.int32)[None, :]
    weights = jnp.where(fine == 2 * target, 0.5, 0.0) + jnp.where(
        (fine == 2 * target + 1) | (fine == 2 * target - 1), 0.25, 0.0
    )

    def restrict_z(rows):
        flat = rows.reshape(-1, nz)
        flat = jnp.pad(flat, ((0, 128 - flat.shape[0]), (0, 0)))
        out = lax.dot_general(
            weights, flat, (((1,), (1,)), ((), ())), precision=lax.Precision.HIGHEST
        )
        return out.reshape(levels, zblock, 128)

    own_part = restrict_z(own)
    edge_part = restrict_z(b_row)
    send = jnp.where(
        odd_b,
        jnp.concatenate([own_part, edge_part], 0),
        jnp.concatenate([edge_part, own_part], 0),
    )
    got = lax.all_to_all(
        send, BOTH, split_axis=0, concat_axis=0, tiled=True, axis_index_groups=columns
    )
    own_got = jnp.where(odd_b, got[:levels], got[levels:])
    edge_got = jnp.where(odd_b, got[levels:], got[:levels])
    half_x = both.shape[1] - 2
    rows = fields * (half_x + 2)
    own_got = own_got[..., : rows * half_y].reshape(levels, zblock, fields, half_x + 2, half_y)
    edge_got = edge_got[..., :rows].reshape(levels, zblock, fields, half_x + 2, 1)
    b_at = jnp.where(odd_b, half_y - 1, 0)
    rest = jnp.where((jnp.arange(half_y) == b_at) & b_valid, edge_got, 0.0)
    total = own_got + rest
    up = total[:-1, :, :, -1:]
    down = total[1:, :, :, :1]
    none = jnp.zeros_like(total[:1, :, :, :1])
    up = jnp.concatenate([none, up], 0)
    down = jnp.concatenate([down, none], 0)
    body = total[:, :, :, 1:-1]
    body = jnp.concatenate(
        [body[:, :, :, :1] + up, body[:, :, :, 1:-1], body[:, :, :, -1:] + down], 3
    )
    coarse_rhs = body.transpose(2, 0, 3, 4, 1).reshape(
        fields, levels * half_x, half_y, zblock
    )[None]
    return (smoothed, coarse_rhs)


def solution(mesh):
    placed = (
        P(None, "level", "brick", None),
        P(None, "level", "brick", None),
        P(None, None, "level", "brick", None),
        P(None, None, "level", "brick", None),
        P(None, "level", "brick", None),
        P("level", "brick", None),
        P(),
    )
    return jax.shard_map(
        shards,
        mesh=mesh,
        in_specs=placed,
        out_specs=(P(None, "level", "brick", None), P("level", None, None, "brick", None)),
        check_vma=False,
    )
```

```python
import jax
import jax.numpy as jnp
from jax import lax
from jax.sharding import PartitionSpec as P


SWEEPS = 4
relax_factor = 0.8
BOTH = ("brick", "level")


def far_pairs(count):
    return [(i, (i + 1) % count) for i in range(1, count, 2)]


def near_pairs(count):
    return [(i, i + 1) for i in range(0, count, 2)]


def both_ways(pairs):
    return pairs + [(b, a) for a, b in pairs]


def split_wide(values):
    high = lax.reduce_precision(values, 8, 7)
    low = values - high
    return high.astype(jnp.bfloat16), low.astype(jnp.bfloat16)


def join_wide(high, low):
    return high.astype(jnp.float32) + low.astype(jnp.float32)


def matvec(rows, cells):
    count = cells.shape[0]
    fields = []
    for outer in range(count):
        total = rows(outer, 0) * cells[0]
        for inner in range(1, count):
            total = total + rows(outer, inner) * cells[inner]
        fields.append(total)
    return jnp.stack(fields)


def along_z(cells):
    zero = jnp.zeros_like(cells[..., :1])
    return jnp.concatenate([cells[..., 1:], zero], -1) + jnp.concatenate([zero, cells[..., :-1]], -1)


def operator(cells, neighbours, block, couple):
    diagonal = matvec(lambda outer, inner: block[inner, outer].astype(jnp.float32), cells)
    coupled = (
        couple[0] * neighbours[0] + couple[1] * neighbours[1] + couple[2] * along_z(cells)
    )
    return diagonal - coupled


def relaxed(cells, neighbours, block, precond, source, couple, keep):
    defect = source - operator(cells, neighbours, block, couple)
    step = matvec(lambda outer, inner: precond[outer, inner].astype(jnp.float32), defect)
    return jnp.where(keep, cells + relax_factor * step, 0.0)


def shards(adjoint, source, block, precond, couple, solid, coarse_owner):
    levels = lax.axis_size("level")
    bricks = lax.axis_size("brick")
    level = lax.axis_index("level")
    brick = lax.axis_index("brick")
    odd_l = level % 2 == 1
    odd_b = brick % 2 == 1
    fields = adjoint.shape[0]
    last = adjoint.shape[1] - 1
    keep = solid == 0

    f_valid = jnp.where(odd_l, level < levels - 1, level > 0)
    b_valid = jnp.where(odd_b, brick < bricks - 1, brick > 0)

    b_route = both_ways(far_pairs(bricks)[:-1])
    f_route = both_ways(far_pairs(levels)[:-1])
    a_groups = [list(pair) for pair in near_pairs(bricks)]
    n_groups = [list(pair) for pair in near_pairs(levels)]
    columns = [
        [b * levels + l for b in pair for l in range(levels)] for pair in far_pairs(bricks)
    ]

    def x_row(values, depth, above):
        low = values[..., depth, :, :]
        high = values[..., last - depth, :, :]
        return jnp.where(above, high, low)

    def y_row(values, depth, above):
        low = values[..., depth, :]
        high = values[..., last - depth, :]
        return jnp.where(above, high, low)

    edge_at = {
        "F": lambda v, d: x_row(v, d, odd_l),
        "N": lambda v, d: x_row(v, d, ~odd_l),
        "A": lambda v, d: y_row(v, d, ~odd_b),
        "B": lambda v, d: y_row(v, d, odd_b),
    }

    def facing(side, strip):
        above = {"F": odd_l, "N": ~odd_l, "A": ~odd_b, "B": odd_b}[side]
        return jnp.where(above, strip[..., last, :], strip[..., 0, :])

    def state_planes(cells, side):
        both = jnp.concatenate([edge_at[side](cells, 0), edge_at[side](cells, 1)], 0)
        high, low = split_wide(both)
        return jnp.concatenate([high, low], 0)

    def fixed_planes(side):
        at = edge_at[side]
        order = (0, 1) if side in "FN" else (1, 0)
        pair = jnp.stack([couple[order[0]], couple[order[1]], couple[2]])
        wide = jnp.concatenate([at(source, 0), at(pair, 0)], 0)
        high, low = split_wide(wide)
        count = fields * fields
        return jnp.concatenate(
            [
                high,
                low,
                at(solid, 0)[None].astype(jnp.bfloat16),
                at(block, 0).reshape((count,) + high.shape[1:]),
                at(precond, 0).reshape((count,) + high.shape[1:]),
            ],
            0,
        )

    n_state = 4 * fields
    n_wide = fields + 3

    def corner_planes(corner):
        high, low = split_wide(corner)
        rows = last + 1
        return jnp.pad(jnp.stack([high, low]), ((0, 0), (0, rows - fields), (0, 0)))

    def corner_of(planes):
        return join_wide(planes[0, :fields], planes[1, :fields])

    def near_state(planes):
        return join_wide(planes[:fields], planes[2 * fields : 3 * fields])

    def deep_state(planes):
        return join_wide(planes[fields : 2 * fields], planes[3 * fields : 4 * fields])

    def exchange(cells, fixed):
        planes = {}
        for side in "FNAB":
            parts = [state_planes(cells, side)]
            if fixed is not None:
                parts.append(fixed[side])
            planes[side] = jnp.concatenate(parts, 0)

        b_got = lax.ppermute(planes["B"], "brick", b_route)
        got = lax.all_gather(planes["A"], "brick", axis_index_groups=a_groups)
        a_got = jnp.where(odd_b, got[0], got[1])
        a_near, a_deep = near_state(a_got), deep_state(a_got)
        b_near, b_deep = near_state(b_got), deep_state(b_got)

        def with_ends(side):
            ends = [corner_planes(facing(side, strip)) for strip in (a_near, b_near)]
            return jnp.concatenate([planes[side]] + ends, 0)

        f_send, n_send = with_ends("F"), with_ends("N")
        f_got = lax.ppermute(f_send, "level", f_route)
        got = lax.all_gather(n_send, "level", axis_index_groups=n_groups)
        n_got = jnp.where(odd_l, got[0], got[1])
        f_near, f_deep = near_state(f_got), deep_state(f_got)
        n_near, n_deep = near_state(n_got), deep_state(n_got)
        fa, fb = corner_of(f_got[-4:-2]), corner_of(f_got[-2:])
        na, nb = corner_of(n_got[-4:-2]), corner_of(n_got[-2:])

        strips = jnp.stack([f_near, n_near, a_near, b_near], 1)
        deep = jnp.stack([f_deep, n_deep, a_deep, b_deep], 1)
        low = jnp.stack(
            [
                jnp.where(odd_b, fa, fb),
                jnp.where(odd_b, na, nb),
                jnp.where(odd_l, na, fa),
                jnp.where(odd_l, nb, fb),
            ],
            1,
        )
        high = jnp.stack(
            [
                jnp.where(odd_b, fb, fa),
                jnp.where(odd_b, nb, na),
                jnp.where(odd_l, fa, na),
                jnp.where(odd_l, fb, nb),
            ],
            1,
        )
        received = {"F": f_got, "N": n_got, "A": a_got, "B": b_got}
        return strips, deep, low, high, received

    def around(strips):
        f, n, a, b = (strips[:, i] for i in range(4))
        x_low, x_high = jnp.where(odd_l, n, f), jnp.where(odd_l, f, n)
        y_low, y_high = jnp.where(odd_b, a, b), jnp.where(odd_b, b, a)
        return x_low, x_high, y_low, y_high

    def own_neighbours(cells, sides):
        x_low, x_high, y_low, y_high = sides
        tall = jnp.concatenate([x_low[:, None], cells, x_high[:, None]], 1)
        wide = jnp.concatenate([y_low[:, :, None], cells, y_high[:, :, None]], 2)
        return tall[:, 2:] + tall[:, :-2], wide[:, :, 2:] + wide[:, :, :-2]

    def inner_edges(cells):
        return jnp.stack([edge_at[side](cells, 0) for side in "FNAB"], 1)

    def strip_neighbours(cells, strips, deep, low, high):
        before = jnp.concatenate([low[:, :, None], strips[:, :, :-1]], 2)
        after = jnp.concatenate([strips[:, :, 1:], high[:, :, None]], 2)
        return deep + inner_edges(cells), before + after

    fixed = {side: fixed_planes(side) for side in "FNAB"}
    cells = adjoint
    ring = None
    for _ in range(SWEEPS // 2):
        strips, deep, low, high, received = exchange(cells, fixed if ring is None else None)
        if ring is None:
            wide = []
            masks = []
            blocks = []
            preconds = []
            for side in "FNAB":
                rest = received[side][n_state:]
                wide.append(join_wide(rest[:n_wide], rest[n_wide : 2 * n_wide]))
                open_cells = rest[2 * n_wide] == 0
                if side == "F":
                    open_cells = open_cells & f_valid
                if side == "B":
                    open_cells = open_cells & b_valid
                masks.append(open_cells)
                start = 2 * n_wide + 1
                count = fields * fields
                shape = (fields, fields) + rest.shape[1:]
                blocks.append(rest[start : start + count].reshape(shape))
                preconds.append(rest[start + count : start + 2 * count].reshape(shape))
            wide = jnp.stack(wide, 1)
            ring = {
                "source": wide[:fields],
                "couple": wide[fields:],
                "keep": jnp.stack(masks),
                "block": jnp.stack(blocks, 2),
                "precond": jnp.stack(preconds, 2),
            }
        first = relaxed(
            cells, own_neighbours(cells, around(strips)), block, precond, source, couple, keep
        )
        strips = relaxed(
            strips,
            strip_neighbours(cells, strips, deep, low, high),
            ring["block"],
            ring["precond"],
            ring["source"],
            ring["couple"],
            ring["keep"],
        )
        cells = relaxed(
            first, own_neighbours(first, around(strips)), block, precond, source, couple, keep
        )
    smoothed = cells

    nothing = jnp.zeros_like(strips)
    inside = own_neighbours(cells, around(nothing))
    residual = jnp.where(keep, source - operator(cells, inside, block, couple), 0.0)
    beyond = jnp.where(ring["keep"], ring["couple"][0] * inner_edges(cells), 0.0)
    x_low, x_high, y_low, y_high = around(beyond)

    def restrict(before, values, after, axis):
        length = values.shape[axis]
        even = lax.slice_in_dim(values, 0, length, 2, axis)
        odd = lax.slice_in_dim(values, 1, length, 2, axis)
        even = jnp.concatenate([jnp.zeros_like(before), even, after], axis)
        odd = jnp.concatenate([before, odd], axis)
        none = jnp.zeros_like(before)
        return (
            0.5 * even
            + 0.25 * jnp.concatenate([odd, none], axis)
            + 0.25 * jnp.concatenate([none, odd], axis)
        )

    along_x = restrict(x_low[:, None], residual, x_high[:, None], 1)
    blank = jnp.zeros_like(y_low[:, :1])
    y_low = restrict(blank, y_low, blank, 1)
    y_high = restrict(blank, y_high, blank, 1)
    both = restrict(y_low[:, :, None], along_x, y_high[:, :, None], 2)
    half_y = both.shape[2] - 2
    below, own, above = both[:, :, 0], both[:, :, 1:-1], both[:, :, -1]
    a_row = jnp.where(odd_b, below, above)
    b_row = jnp.where(odd_b, above, below)
    got = lax.all_gather(a_row, "brick", axis_index_groups=a_groups)
    a_got = jnp.where(odd_b, got[0], got[1])
    at_row = lax.broadcasted_iota(jnp.int32, (half_y, 1), 0)
    a_at = jnp.where(odd_b, 0, half_y - 1)
    own = own + jnp.where(at_row == a_at, a_got[:, :, None], 0.0)

    nz = adjoint.shape[3]
    zblock = nz // (2 * levels)
    slots = jnp.arange(levels, dtype=jnp.int32)
    inverse = jnp.sum(jnp.where(coarse_owner[None, :] == slots[:, None], slots[None, :], 0), axis=1)
    target = (inverse[:, None] * zblock + jnp.arange(zblock, dtype=jnp.int32)[None, :]).reshape(-1, 1)
    fine = jnp.arange(nz, dtype=jnp.int32)[None, :]
    weights = jnp.where(fine == 2 * target, 0.5, 0.0) + jnp.where(
        (fine == 2 * target + 1) | (fine == 2 * target - 1), 0.25, 0.0
    )

    def restrict_z(rows):
        flat = rows.reshape(-1, nz)
        flat = jnp.pad(flat, ((0, 128 - flat.shape[0]), (0, 0)))
        out = lax.dot_general(
            weights, flat, (((1,), (1,)), ((), ())), precision=lax.Precision.HIGHEST
        )
        return out.reshape(levels, zblock, 128)

    own_part = restrict_z(own)
    edge_part = restrict_z(b_row)
    send = jnp.where(
        odd_b,
        jnp.concatenate([own_part, edge_part], 0),
        jnp.concatenate([edge_part, own_part], 0),
    )
    got = lax.all_to_all(
        send, BOTH, split_axis=0, concat_axis=0, tiled=True, axis_index_groups=columns
    )
    own_got = jnp.where(odd_b, got[:levels], got[levels:])
    edge_got = jnp.where(odd_b, got[levels:], got[:levels])
    half_x = both.shape[1] - 2
    rows = fields * (half_x + 2)
    own_got = own_got[..., : rows * half_y].reshape(levels, zblock, fields, half_x + 2, half_y)
    edge_got = edge_got[..., :rows].reshape(levels, zblock, fields, half_x + 2, 1)
    b_at = jnp.where(odd_b, half_y - 1, 0)
    rest = jnp.where((jnp.arange(half_y) == b_at) & b_valid, edge_got, 0.0)
    total = own_got + rest
    up = total[:-1, :, :, -1:]
    down = total[1:, :, :, :1]
    none = jnp.zeros_like(total[:1, :, :, :1])
    up = jnp.concatenate([none, up], 0)
    down = jnp.concatenate([down, none], 0)
    body = total[:, :, :, 1:-1]
    body = jnp.concatenate(
        [body[:, :, :, :1] + up, body[:, :, :, 1:-1], body[:, :, :, -1:] + down], 3
    )
    coarse_rhs = body.transpose(2, 0, 3, 4, 1).reshape(
        fields, levels * half_x, half_y, zblock
    )[None]
    return (smoothed, coarse_rhs)


def solution(mesh):
    placed = (
        P(None, "level", "brick", None),
        P(None, "level", "brick", None),
        P(None, None, "level", "brick", None),
        P(None, None, "level", "brick", None),
        P(None, "level", "brick", None),
        P("level", "brick", None),
        P(),
    )
    return jax.shard_map(
        shards,
        mesh=mesh,
        in_specs=placed,
        out_specs=(P(None, "level", "brick", None), P("level", None, None, "brick", None)),
        check_vma=False,
    )
```

```python
import jax
import jax.numpy as jnp
from jax import lax
from jax.sharding import PartitionSpec as P


SWEEPS = 4
relax_factor = 0.8
BOTH = ("brick", "level")


def far_pairs(count):
    return [(i, (i + 1) % count) for i in range(1, count, 2)]


def near_pairs(count):
    return [(i, i + 1) for i in range(0, count, 2)]


def both_ways(pairs):
    return pairs + [(b, a) for a, b in pairs]


def split_wide(values):
    high = lax.reduce_precision(values, 8, 7)
    low = values - high
    return high.astype(jnp.bfloat16), low.astype(jnp.bfloat16)


def join_wide(high, low):
    return high.astype(jnp.float32) + low.astype(jnp.float32)


def matvec(rows, cells):
    count = cells.shape[0]
    fields = []
    for outer in range(count):
        total = rows(outer, 0) * cells[0]
        for inner in range(1, count):
            total = total + rows(outer, inner) * cells[inner]
        fields.append(total)
    return jnp.stack(fields)


def along_z(cells):
    zero = jnp.zeros_like(cells[..., :1])
    return jnp.concatenate([cells[..., 1:], zero], -1) + jnp.concatenate([zero, cells[..., :-1]], -1)


def operator(cells, neighbours, block, couple):
    diagonal = matvec(lambda outer, inner: block[inner, outer].astype(jnp.float32), cells)
    coupled = (
        couple[0] * neighbours[0] + couple[1] * neighbours[1] + couple[2] * along_z(cells)
    )
    return diagonal - coupled


def shards(adjoint, source, block, precond, couple, solid, coarse_owner):
    levels = lax.axis_size("level")
    bricks = lax.axis_size("brick")
    level = lax.axis_index("level")
    brick = lax.axis_index("brick")
    odd_l = level % 2 == 1
    odd_b = brick % 2 == 1
    fields = adjoint.shape[0]
    last = adjoint.shape[1] - 1
    keep = solid == 0

    b_valid = jnp.where(odd_b, brick < bricks - 1, brick > 0)
    b_route = both_ways(far_pairs(bricks)[:-1])
    f_route = both_ways(far_pairs(levels)[:-1])
    a_groups = [list(pair) for pair in near_pairs(bricks)]
    n_groups = [list(pair) for pair in near_pairs(levels)]
    columns = [
        [b * levels + l for b in pair for l in range(levels)] for pair in far_pairs(bricks)
    ]

    def x_row(values, depth, above):
        low = values[..., depth, :, :]
        high = values[..., last - depth, :, :]
        return jnp.where(above, high, low)

    def y_row(values, depth, above):
        low = values[..., depth, :]
        high = values[..., last - depth, :]
        return jnp.where(above, high, low)

    edge_at = {
        "F": lambda v, d: x_row(v, d, odd_l),
        "N": lambda v, d: x_row(v, d, ~odd_l),
        "A": lambda v, d: y_row(v, d, ~odd_b),
        "B": lambda v, d: y_row(v, d, odd_b),
    }

    def facing(side, strip):
        above = {"F": odd_l, "N": ~odd_l, "A": ~odd_b, "B": odd_b}[side]
        return jnp.where(above, strip[..., last, :], strip[..., 0, :])

    def planes_of(wide):
        high, low = split_wide(wide)
        return jnp.concatenate([high, low], 0)

    def wide_of(planes, count):
        return join_wide(planes[:count], planes[count : 2 * count])

    def corner_planes(corner):
        high, low = split_wide(corner)
        rows = last + 1
        return jnp.pad(jnp.stack([high, low]), ((0, 0), (0, rows - fields), (0, 0)))

    def corner_of(planes):
        return join_wide(planes[0, :fields], planes[1, :fields])

    def preconditioned(precond, values):
        return matvec(lambda outer, inner: precond[outer, inner].astype(jnp.float32), values)

    open_couple = jnp.where(keep, couple, 0.0)
    precond_edge = {side: edge_at[side](precond, 0) for side in "FNAB"}
    keep_edge = {side: edge_at[side](keep, 0) for side in "FNAB"}

    def fixed_planes(side):
        at = edge_at[side]
        order = (0, 1) if side in "FN" else (1, 0)
        pair = jnp.stack([at(open_couple[axis], 0) for axis in order])
        flat = precond_edge[side].reshape((fields * fields,) + pair.shape[1:])
        return jnp.concatenate([planes_of(pair), flat], 0)

    def state_planes(cells, defect, side):
        edge = edge_at[side](cells, 0)
        step = preconditioned(precond_edge[side], edge_at[side](defect, 0))
        base = jnp.where(keep_edge[side], edge + relax_factor * step, 0.0)
        return planes_of(jnp.concatenate([edge, base], 0))

    n_state = 4 * fields
    fixed_count = 4 + fields * fields
    row_at = lax.broadcasted_iota(jnp.int32, (last + 1, 1), 0)

    def across(low, high):
        return jnp.where(row_at == 0, low, jnp.where(row_at == last, high, 0.0))

    def exchange(cells, defect, fixed):
        def planes(side, state):
            return [state_planes(cells, state, side)] + ([fixed[side]] if fixed else [])

        def opened(got):
            wide = wide_of(got, 2 * fields)
            return wide[:fields], wide[fields:], got[n_state : n_state + fixed_count]

        b_send = jnp.concatenate(planes("B", defect), 0)
        a_send = jnp.concatenate(planes("A", defect), 0)
        b_got = lax.ppermute(b_send, "brick", b_route)
        got = lax.all_gather(a_send, "brick", axis_index_groups=a_groups)
        a_got = jnp.where(odd_b, got[0], got[1])
        a_near, a_base, a_fixed = opened(a_got)
        b_near, b_base, b_fixed = opened(b_got)
        y_low = jnp.where(odd_b, a_near, b_near)
        y_high = jnp.where(odd_b, b_near, a_near)
        defect = defect + couple[1] * across(y_low[:, :, None], y_high[:, :, None])

        def with_ends(side):
            ends = [corner_planes(facing(side, strip)) for strip in (a_near, b_near)]
            return jnp.concatenate(planes(side, defect) + ends, 0)

        f_send, n_send = with_ends("F"), with_ends("N")
        f_got = lax.ppermute(f_send, "level", f_route)
        got = lax.all_gather(n_send, "level", axis_index_groups=n_groups)
        n_got = jnp.where(odd_l, got[0], got[1])
        f_near, f_base, f_fixed = opened(f_got)
        n_near, n_base, n_fixed = opened(n_got)
        x_low = jnp.where(odd_l, n_near, f_near)[:, None]
        x_high = jnp.where(odd_l, f_near, n_near)[:, None]
        blank = jnp.zeros_like(cells[:, 2:])
        defect = defect + couple[0] * jnp.concatenate([x_low, blank, x_high], 1)

        none = jnp.zeros_like(f_near)
        ends = [none, none]
        for at in (-4, -2):
            far, near = corner_of(f_got[at:][:2]), corner_of(n_got[at:][:2])
            low, high = jnp.where(odd_l, near, far), jnp.where(odd_l, far, near)
            ends.append(across(low[:, None], high[:, None]))
        bases = jnp.stack([f_base, n_base, a_base, b_base], 1)
        return defect, bases, jnp.stack(ends, 1), [f_fixed, n_fixed, a_fixed, b_fixed]

    def around(strips):
        f, n, a, b = (strips[:, i] for i in range(4))
        x_low, x_high = jnp.where(odd_l, n, f), jnp.where(odd_l, f, n)
        y_low, y_high = jnp.where(odd_b, a, b), jnp.where(odd_b, b, a)
        return x_low, x_high, y_low, y_high

    def own_neighbours(cells, sides):
        x_low, x_high, y_low, y_high = sides
        tall = jnp.concatenate([x_low[:, None], cells, x_high[:, None]], 1)
        wide = jnp.concatenate([y_low[:, :, None], cells, y_high[:, :, None]], 2)
        return tall[:, 2:] + tall[:, :-2], wide[:, :, 2:] + wide[:, :, :-2]

    def inner_edges(cells):
        return jnp.stack([edge_at[side](cells, 0) for side in "FNAB"], 1)

    def defect_of(cells, strips):
        return source - operator(cells, own_neighbours(cells, around(strips)), block, couple)

    def relaxed(cells, defect):
        step = preconditioned(precond, defect)
        return jnp.where(keep, cells + relax_factor * step, 0.0)

    cells = adjoint
    nothing = jnp.zeros((fields, 4) + adjoint.shape[2:], jnp.float32)
    ring = None
    for _ in range(SWEEPS // 2):
        fixed = None if ring else {side: fixed_planes(side) for side in "FNAB"}
        defect = defect_of(cells, nothing)
        defect, bases, ends, received = exchange(cells, defect, fixed)
        if ring is None:
            pairs = jnp.stack([wide_of(got, 2) for got in received], 1)
            shape = (fields, fields) + adjoint.shape[2:]
            ring = {
                "normal": pairs[0],
                "tangent": pairs[1],
                "precond": jnp.stack([got[4:].reshape(shape) for got in received], 2),
            }
        first = relaxed(cells, defect)
        missing = ring["normal"] * inner_edges(cells) + ring["tangent"] * ends
        strips = bases + relax_factor * preconditioned(ring["precond"], missing)
        cells = relaxed(first, defect_of(first, strips))
    smoothed = cells

    residual = jnp.where(keep, defect_of(cells, nothing), 0.0)
    beyond = ring["normal"] * inner_edges(cells)
    x_low, x_high, y_low, y_high = around(beyond)

    def restrict(before, values, after, axis):
        length = values.shape[axis]
        even = lax.slice_in_dim(values, 0, length, 2, axis)
        odd = lax.slice_in_dim(values, 1, length, 2, axis)
        even = jnp.concatenate([jnp.zeros_like(before), even, after], axis)
        odd = jnp.concatenate([before, odd], axis)
        none = jnp.zeros_like(before)
        return (
            0.5 * even
            + 0.25 * jnp.concatenate([odd, none], axis)
            + 0.25 * jnp.concatenate([none, odd], axis)
        )

    along_x = restrict(x_low[:, None], residual, x_high[:, None], 1)
    blank = jnp.zeros_like(y_low[:, :1])
    y_low = restrict(blank, y_low, blank, 1)
    y_high = restrict(blank, y_high, blank, 1)
    both = restrict(y_low[:, :, None], along_x, y_high[:, :, None], 2)
    half_y = both.shape[2] - 2
    below, own, above = both[:, :, 0], both[:, :, 1:-1], both[:, :, -1]
    a_row = jnp.where(odd_b, below, above)
    b_row = jnp.where(odd_b, above, below)
    got = lax.all_gather(a_row, "brick", axis_index_groups=a_groups)
    a_got = jnp.where(odd_b, got[0], got[1])
    at_row = lax.broadcasted_iota(jnp.int32, (half_y, 1), 0)
    a_at = jnp.where(odd_b, 0, half_y - 1)
    own = own + jnp.where(at_row == a_at, a_got[:, :, None], 0.0)

    nz = adjoint.shape[3]
    zblock = nz // (2 * levels)
    slots = jnp.arange(levels, dtype=jnp.int32)
    inverse = jnp.sum(jnp.where(coarse_owner[None, :] == slots[:, None], slots[None, :], 0), axis=1)
    target = (inverse[:, None] * zblock + jnp.arange(zblock, dtype=jnp.int32)[None, :]).reshape(-1, 1)
    fine = jnp.arange(nz, dtype=jnp.int32)[None, :]
    weights = jnp.where(fine == 2 * target, 0.5, 0.0) + jnp.where(
        (fine == 2 * target + 1) | (fine == 2 * target - 1), 0.25, 0.0
    )

    def restrict_z(rows):
        flat = rows.reshape(-1, nz)
        flat = jnp.pad(flat, ((0, 128 - flat.shape[0]), (0, 0)))
        out = lax.dot_general(
            weights, flat, (((1,), (1,)), ((), ())), precision=lax.Precision.HIGHEST
        )
        return out.reshape(levels, zblock, 128)

    own_part = restrict_z(own)
    edge_part = restrict_z(b_row)
    send = jnp.where(
        odd_b,
        jnp.concatenate([own_part, edge_part], 0),
        jnp.concatenate([edge_part, own_part], 0),
    )
    got = lax.all_to_all(
        send, BOTH, split_axis=0, concat_axis=0, tiled=True, axis_index_groups=columns
    )
    own_got = jnp.where(odd_b, got[:levels], got[levels:])
    edge_got = jnp.where(odd_b, got[levels:], got[:levels])
    half_x = both.shape[1] - 2
    rows = fields * (half_x + 2)
    own_got = own_got[..., : rows * half_y].reshape(levels, zblock, fields, half_x + 2, half_y)
    edge_got = edge_got[..., :rows].reshape(levels, zblock, fields, half_x + 2, 1)
    b_at = jnp.where(odd_b, half_y - 1, 0)
    rest = jnp.where((jnp.arange(half_y) == b_at) & b_valid, edge_got, 0.0)
    total = own_got + rest
    up = total[:-1, :, :, -1:]
    down = total[1:, :, :, :1]
    none = jnp.zeros_like(total[:1, :, :, :1])
    up = jnp.concatenate([none, up], 0)
    down = jnp.concatenate([down, none], 0)
    body = total[:, :, :, 1:-1]
    body = jnp.concatenate(
        [body[:, :, :, :1] + up, body[:, :, :, 1:-1], body[:, :, :, -1:] + down], 3
    )
    coarse_rhs = body.transpose(2, 0, 3, 4, 1).reshape(
        fields, levels * half_x, half_y, zblock
    )[None]
    return (smoothed, coarse_rhs)


def solution(mesh):
    placed = (
        P(None, "level", "brick", None),
        P(None, "level", "brick", None),
        P(None, None, "level", "brick", None),
        P(None, None, "level", "brick", None),
        P(None, "level", "brick", None),
        P("level", "brick", None),
        P(),
    )
    return jax.shard_map(
        shards,
        mesh=mesh,
        in_specs=placed,
        out_specs=(P(None, "level", "brick", None), P("level", None, None, "brick", None)),
        check_vma=False,
    )
```

```python
import functools

import jax
import jax.numpy as jnp
from jax import lax
from jax.experimental import pallas as pl
from jax.experimental.pallas import tpu as pltpu
from jax.sharding import PartitionSpec as P


relax_factor = 0.8
BOTH = ("brick", "level")
FIELDS = 5
SIDE = 8
TILE = SIDE * SIDE
LANES = 128
STATE = 4 * FIELDS
FIXED = 4 + FIELDS * FIELDS
HALF = SIDE // 2
OUTER = HALF + 2
f32 = jnp.float32


def far_pairs(count):
    return [(i, i + 1) for i in range(1, count - 1, 2)]


def near_pairs(count):
    return [[i, i + 1] for i in range(0, count, 2)]


def both_ways(pairs):
    return pairs + [(b, a) for a, b in pairs]


def iota(axis):
    return lax.broadcasted_iota(jnp.int32, (SIDE, LANES), axis)


def tile(ref, field, x):
    return ref[pl.ds((field * SIDE + x) * SIDE, SIDE), :]


def y_edge(ref, field, y):
    return ref[pl.ds(field * TILE + y, SIDE, stride=SIDE), :]


def put(ref, index, value):
    high = value.astype(jnp.bfloat16)
    ref[index] = high
    return (value - high.astype(f32)).astype(jnp.bfloat16)


def put_wide(ref, start, count, index, value):
    ref[start + count + index] = put(ref, start + index, value)


def wide(planes, start, count, index):
    return planes(start + index).astype(f32) + planes(start + count + index).astype(f32)


def shifted(value, axis):
    size = value.shape[axis]
    at = iota(axis)
    before = jnp.where(at == 0, 0.0, pltpu.roll(value, 1, axis))
    after = jnp.where(at == size - 1, 0.0, pltpu.roll(value, size - 1, axis))
    return before + after


def defect_tile(s, halo, source, block, couple, x):
    x_low, x_high, y_low, y_high = halo
    here = [tile(s, field, x) for field in range(FIELDS)]
    c0, c1, c2 = (tile(couple, axis, x) for axis in range(3))
    row = iota(0)
    out = []
    for outer in range(FIELDS):
        total = block[0, outer, x].astype(f32) * here[0]
        for inner in range(1, FIELDS):
            total = total + block[inner, outer, x].astype(f32) * here[inner]
        near_y = shifted(here[outer], 0)
        if y_low is not None:
            near_y = near_y + jnp.where(row == 0, y_low(outer, x), 0.0)
            near_y = near_y + jnp.where(row == SIDE - 1, y_high(outer, x), 0.0)
        coupled = c1 * near_y + c2 * shifted(here[outer], 1)
        near_x = None
        if x > 0:
            near_x = tile(s, outer, x - 1)
        elif x_low is not None:
            near_x = x_low(outer)
        other = None
        if x < SIDE - 1:
            other = tile(s, outer, x + 1)
        elif x_high is not None:
            other = x_high(outer)
        both = [v for v in (near_x, other) if v is not None]
        coupled = coupled + c0 * (both[0] if len(both) == 1 else both[0] + both[1])
        out.append(tile(source, outer, x) - (total - coupled))
    return out


def stepped(precond, defect):
    out = []
    for outer in range(FIELDS):
        total = precond(outer, 0) * defect[0]
        for inner in range(1, FIELDS):
            total = total + precond(outer, inner) * defect[inner]
        out.append(total)
    return out


def sweep(s, halo, ins, out):
    for x in range(SIDE):
        defect = defect_tile(s, halo, ins.source, ins.block, ins.couple, x)
        step = stepped(lambda o, i: ins.precond[o, i, x].astype(f32), defect)
        keep = ins.solid[pl.ds(x * SIDE, SIDE), :] == 0
        for field in range(FIELDS):
            value = jnp.where(keep, tile(s, field, x) + relax_factor * step[field], 0.0)
            out[pl.ds((field * SIDE + x) * SIDE, SIDE), :] = value


class Cells:
    def __init__(self, source, block, precond, couple, solid):
        self.source, self.block, self.precond = source, block, precond
        self.couple, self.solid = couple, solid


def y_state(s, ins, odd_b, sends, d, keeps, pf, opens):
    none = (None,) * 4
    for x in range(SIDE):
        defect = defect_tile(s, none, ins.source, ins.block, ins.couple, x)
        for field in range(FIELDS):
            d[pl.ds((field * SIDE + x) * SIDE, SIDE), :] = defect[field]
    for side, send in zip("BA", sends):
        above = odd_b if side == "B" else 1 - odd_b
        y = above * (SIDE - 1)
        p = [[y_edge(pf, o * FIELDS + i, y) for i in range(FIELDS)] for o in range(FIELDS)]
        step = stepped(lambda o, i: p[o][i], [y_edge(d, i, y) for i in range(FIELDS)])
        keep = y_edge(keeps, 0, y) == 0.0
        for field in range(FIELDS):
            edge = y_edge(s, field, y)
            put_wide(send, 0, 2 * FIELDS, field, edge)
            base = jnp.where(keep, edge + relax_factor * step[field], 0.0)
            put_wide(send, 0, 2 * FIELDS, FIELDS + field, base)
        if opens is not None:
            put_wide(send, STATE, 2, 0, y_edge(opens, 1, y))
            put_wide(send, STATE, 2, 1, y_edge(opens, 0, y))
            for o in range(FIELDS):
                for i in range(FIELDS):
                    send[STATE + 4 + o * FIELDS + i] = p[o][i].astype(jnp.bfloat16)


def fill(ins, pf, keeps, opens):
    for x in range(SIDE):
        solid = ins.solid[pl.ds(x * SIDE, SIDE), :]
        keeps[pl.ds(x * SIDE, SIDE), :] = solid.astype(f32)
        if opens is not None:
            for axis in range(2):
                rows = pl.ds((axis * SIDE + x) * SIDE, SIDE)
                opens[rows, :] = jnp.where(solid == 0, tile(ins.couple, axis, x), 0.0)
        for o in range(FIELDS):
            for i in range(FIELDS):
                rows = pl.ds(((o * FIELDS + i) * SIDE + x) * SIDE, SIDE)
                pf[rows, :] = ins.precond[o, i, x].astype(f32)


def first_kernel(
    odd, s_hbm, source_hbm, block_hbm, precond_hbm, couple_hbm, solid_hbm,
    s, source, block, precond, couple, solid, b_send, a_send,
    d, keeps, pf, opens, done,
):
    pairs = (
        (solid_hbm, solid), (couple_hbm, couple), (s_hbm, s),
        (precond_hbm, precond), (source_hbm, source), (block_hbm, block),
    )
    copies = [pltpu.make_async_copy(a, b, done.at[k]) for k, (a, b) in enumerate(pairs)]
    for copy in copies:
        copy.start()
    for copy in copies[:4]:
        copy.wait()
    ins = Cells(source, block, precond, couple, solid)
    fill(ins, pf, keeps, opens)
    for copy in copies[4:]:
        copy.wait()
    y_state(s, ins, odd[1], (b_send, a_send), d, keeps, pf, opens)


def y_halos(odd_b, b_got, a_got, low, high):
    partner = 1 - odd_b
    for field in range(FIELDS):
        a = wide(lambda k: a_got[partner, k], 0, 2 * FIELDS, field)
        b = wide(lambda k: b_got[k], 0, 2 * FIELDS, field)
        is_odd = odd_b == 1
        low[field] = jnp.where(is_odd, a, b)
        high[field] = jnp.where(is_odd, b, a)


def row_of(ref, field, x):
    return jnp.broadcast_to(ref[field, pl.ds(x, 1), :], (SIDE, LANES))


def second_kernel(
    fixed, odd, s, source, block, precond, couple, solid, b_got, a_got, f_send, n_send, low, high, flat
):
    ins = Cells(source, block, precond, couple, solid)
    odd_l, odd_b = odd[0], odd[1]
    is_odd = odd_l == 1
    y_halos(odd_b, b_got, a_got, low, high)
    halo = (None, None, lambda f, x: row_of(low, f, x), lambda f, x: row_of(high, f, x))
    ends = (0, SIDE - 1)
    edges, bases, pairs = [], [], []
    for x in ends:
        defect = defect_tile(s, halo, source, block, couple, x)
        step = stepped(lambda o, i: precond[o, i, x].astype(f32), defect)
        keep = solid[pl.ds(x * SIDE, SIDE), :] == 0
        edge = [tile(s, field, x) for field in range(FIELDS)]
        edges.append(edge)
        bases.append([jnp.where(keep, e + relax_factor * t, 0.0) for e, t in zip(edge, step)])
        pairs.append([jnp.where(keep, tile(couple, axis, x), 0.0) for axis in range(2)])
    for send, low_side in ((f_send, ~is_odd), (n_send, is_odd)):
        for field in range(FIELDS):
            put_wide(send, 0, 2 * FIELDS, field, jnp.where(low_side, edges[0][field], edges[1][field]))
            base = jnp.where(low_side, bases[0][field], bases[1][field])
            put_wide(send, 0, 2 * FIELDS, FIELDS + field, base)
        count = STATE
        if fixed:
            for axis in range(2):
                pair = jnp.where(low_side, pairs[0][axis], pairs[1][axis])
                put_wide(send, STATE, 2, axis, pair)
            for o in range(FIELDS):
                for i in range(FIELDS):
                    at_low = precond[o, i, 0].astype(f32)
                    at_high = precond[o, i, SIDE - 1].astype(f32)
                    value = jnp.where(low_side, at_low, at_high)
                    send[STATE + 4 + o * FIELDS + i] = value.astype(jnp.bfloat16)
            count += FIXED
        x = jnp.where(low_side, 0, SIDE - 1)
        for index, a_side in enumerate((True, False)):
            flat[...] = jnp.zeros((SIDE, LANES), f32)
            for field in range(FIELDS):
                at_low = low[field, pl.ds(x, 1), :]
                at_high = high[field, pl.ds(x, 1), :]
                low_is_it = (odd_b == 1) if a_side else (odd_b == 0)
                flat[pl.ds(field, 1), :] = jnp.where(low_is_it, at_low, at_high)
            put_wide(send, count + 2 * index, 1, 0, flat[...])


def ring_into(odd, s, got, fixed, low, high, x_low, x_high, corners):
    odd_l, odd_b = odd[0], odd[1]
    is_odd_l, is_odd_b = odd_l == 1, odd_b == 1
    row = iota(0)
    tail = STATE + (FIXED if got["fixed"] else 0)
    for k, (name, start) in enumerate((("F", tail), ("F", tail + 2), ("N", tail), ("N", tail + 2))):
        corners[k] = wide(got[name], start, 1, 0)
    rings = {}
    for side in "FNAB":
        planes, kept = got[side], fixed[side]
        normal = wide(kept, STATE, 2, 0)
        missing = []
        if side in "FN":
            above = odd_l if side == "F" else 1 - odd_l
            for field in range(FIELDS):
                inner = jnp.where(above == 1, tile(s, field, SIDE - 1), tile(s, field, 0))
                missing.append(normal * inner)
        else:
            above = odd_b if side == "B" else 1 - odd_b
            tangent = wide(kept, STATE, 2, 1)
            far, near = (0, 2) if side == "A" else (1, 3)
            for field in range(FIELDS):
                inner = y_edge(s, field, above * (SIDE - 1))
                far_row = row_of(corners, far, field)
                near_row = row_of(corners, near, field)
                first = jnp.where(is_odd_l, near_row, far_row)
                final = jnp.where(is_odd_l, far_row, near_row)
                ends = jnp.where(row == 0, first, jnp.where(row == SIDE - 1, final, 0.0))
                missing.append(normal * inner + tangent * ends)
        step = stepped(lambda o, i: kept(STATE + 4 + o * FIELDS + i).astype(f32), missing)
        rings[side] = [
            wide(planes, 0, 2 * FIELDS, FIELDS + field) + relax_factor * step[field]
            for field in range(FIELDS)
        ]
    for field in range(FIELDS):
        f, n, a, b = (rings[side][field] for side in "FNAB")
        x_low[field] = jnp.where(is_odd_l, n, f)
        x_high[field] = jnp.where(is_odd_l, f, n)
        low[field] = jnp.where(is_odd_b, a, b)
        high[field] = jnp.where(is_odd_b, b, a)


def two_sweeps(odd, s, ins, got, fixed, middle, out, halos):
    low, high, x_low, x_high, corners = halos
    odd_l, odd_b = odd[0], odd[1]
    is_odd_l = odd_l == 1
    y_halos(odd_b, *got["y"], low, high)
    for field in range(FIELDS):
        f = wide(got["F"], 0, 2 * FIELDS, field)
        n = wide(got["N"], 0, 2 * FIELDS, field)
        x_low[field] = jnp.where(is_odd_l, n, f)
        x_high[field] = jnp.where(is_odd_l, f, n)
    halo = (
        lambda field: x_low[field],
        lambda field: x_high[field],
        lambda field, x: row_of(low, field, x),
        lambda field, x: row_of(high, field, x),
    )
    sweep(s, halo, ins, middle)
    ring_into(odd, s, got, fixed, low, high, x_low, x_high, corners)
    sweep(middle, halo, ins, out)


def readers(odd, f_got, n_got, b_got, a_got):
    l, b = 1 - odd[0], 1 - odd[1]
    return {
        "F": lambda k: f_got[k],
        "N": lambda k: n_got[l, k],
        "A": lambda k: a_got[b, k],
        "B": lambda k: b_got[k],
    }


def third_kernel(
    odd, s, source, block, precond, couple, solid, f_got, n_got, b_got, a_got,
    out, b_send, a_send,
    middle, d, keeps, pf, low, high, x_low, x_high, corners,
):
    ins = Cells(source, block, precond, couple, solid)
    got = readers(odd, f_got, n_got, b_got, a_got)
    fixed = dict(got)
    got["fixed"], got["y"] = True, (b_got, a_got)
    two_sweeps(odd, s, ins, got, fixed, middle, out, (low, high, x_low, x_high, corners))
    fill(ins, pf, keeps, None)
    y_state(out, ins, odd[1], (b_send, a_send), d, keeps, pf, None)


def last_kernel(
    odd, s, source, block, precond, couple, solid, f_got, n_got, b_got, a_got, f_old, n_old, b_old, a_old,
    out, own, a_row, b_row,
    middle, low, high, x_low, x_high, corners, grid, below, above,
):
    ins = Cells(source, block, precond, couple, solid)
    got = readers(odd, f_got, n_got, b_got, a_got)
    fixed = readers(odd, f_old, n_old, b_old, a_old)
    got["fixed"], got["y"] = False, (b_got, a_got)
    two_sweeps(odd, s, ins, got, fixed, middle, out, (low, high, x_low, x_high, corners))
    odd_l, odd_b = odd[0], odd[1]
    is_odd_l, is_odd_b = odd_l == 1, odd_b == 1
    none = (None,) * 4
    for x in range(SIDE):
        defect = defect_tile(out, none, source, block, couple, x)
        keep = solid[pl.ds(x * SIDE, SIDE), :] == 0
        for field in range(FIELDS):
            rows = pl.ds((field * SIDE + x) * SIDE, SIDE)
            middle[rows, :] = jnp.where(keep, defect[field], 0.0)
    normal = {side: wide(fixed[side], STATE, 2, 0) for side in "FNAB"}
    row = iota(0)
    for field in range(FIELDS):
        y_at_a, y_at_b = (1 - odd_b) * (SIDE - 1), odd_b * (SIDE - 1)
        a = normal["A"] * y_edge(out, field, y_at_a)
        b = normal["B"] * y_edge(out, field, y_at_b)
        for ref, beyond in ((below, jnp.where(is_odd_b, a, b)), (above, jnp.where(is_odd_b, b, a))):
            even = 0.5 * beyond + 0.25 * shifted(beyond, 0)
            ref[pl.ds(field * OUTER, 1), :] = jnp.zeros((1, LANES), f32)
            for k in range(HALF):
                ref[pl.ds(field * OUTER + 1 + k, 1), :] = even[2 * k : 2 * k + 1]
            ref[pl.ds(field * OUTER + OUTER - 1, 1), :] = 0.25 * beyond[SIDE - 1 :]
    for field in range(FIELDS):
        first, final = tile(out, field, 0), tile(out, field, SIDE - 1)
        f = normal["F"] * jnp.where(is_odd_l, final, first)
        n = normal["N"] * jnp.where(is_odd_l, first, final)
        fine = [tile(middle, field, x) for x in range(SIDE)]
        before, after = jnp.where(is_odd_l, n, f), jnp.where(is_odd_l, f, n)
        coarse = [0.25 * before]
        for k in range(HALF):
            earlier = fine[2 * k - 1] if k else before
            coarse.append(0.5 * fine[2 * k] + 0.25 * (fine[2 * k + 1] + earlier))
        coarse.append(0.5 * after + 0.25 * fine[SIDE - 1])
        for k in range(OUTER):
            value = coarse[k]
            index = field * OUTER + k
            under = below[pl.ds(index, 1), :]
            even = 0.5 * value + 0.25 * shifted(value, 0)
            even = even + jnp.where(row == 0, jnp.broadcast_to(0.25 * under, (SIDE, LANES)), 0.0)
            grid[pl.ds(index * SIDE, SIDE), :] = even
            over = 0.5 * above[pl.ds(index, 1), :] + 0.25 * value[SIDE - 1 :]
            a_row[pl.ds(index, 1), :] = jnp.where(is_odd_b, 0.25 * under, over)
            b_row[pl.ds(index, 1), :] = jnp.where(is_odd_b, over, 0.25 * under)
    count = FIELDS * OUTER
    own[pl.ds(0, count * HALF), :] = grid[pl.ds(0, count * HALF, stride=2), :]
    own[pl.ds(count * HALF, LANES - count * HALF), :] = jnp.zeros((LANES - count * HALF, LANES), f32)
    b_row[pl.ds(count, LANES - count), :] = jnp.zeros((LANES - count, LANES), f32)
    a_row[pl.ds(count, 2), :] = jnp.zeros((2, LANES), f32)


def send_kernel(odd, weights, own, a_got, b_row, send, rows):
    odd_b = odd[1]
    count = FIELDS * OUTER
    rows[...] = own[...]
    at = pl.ds((1 - odd_b) * (HALF - 1), count, stride=HALF)
    rows[at, :] = rows[at, :] + a_got[1 - odd_b, pl.ds(0, count), :]

    values = jnp.concatenate([rows[...], b_row[...]], 0)
    size = weights.shape[0]
    total = jnp.zeros((size, 2 * LANES), f32)
    for _ in range(3):
        part = values.astype(jnp.bfloat16)
        values = values - part.astype(f32)
        total = total + lax.dot_general(
            weights[...], part, (((1,), (1,)), ((), ())), preferred_element_type=f32
        )
    send[pl.ds(pl.multiple_of((1 - odd_b) * size, size), size), :] = total[:, :LANES]
    send[pl.ds(pl.multiple_of(odd_b * size, size), size), :] = total[:, LANES:]


def call(kernel, outs, scratch, *args, resident=True):
    space = pltpu.VMEM if resident else pltpu.HBM
    args = [pltpu.with_memory_space_constraint(arg, space) for arg in args]
    copies = [] if resident else [pltpu.SemaphoreType.DMA((len(args),))]

    def body(*refs):
        kernel(tuple(lax.rem(lax.axis_index(axis), 2) for axis in ("level", "brick")), *refs)

    return pl.pallas_call(
        body,
        out_shape=[pltpu.VMEM(shape, dtype) for shape, dtype in outs],
        in_specs=[pl.BlockSpec(memory_space=space)] * len(args),
        out_specs=[pl.BlockSpec(memory_space=pltpu.VMEM)] * len(outs),
        scratch_shapes=[pltpu.VMEM(shape, f32) for shape in scratch] + copies,
        compiler_params=pltpu.CompilerParams(vmem_limit_bytes=16 * 1024 * 1024),
    )(*args)


def shards(adjoint, source, block, precond, couple, solid, coarse_owner):
    levels = lax.axis_size("level")
    bricks = lax.axis_size("brick")
    brick = lax.axis_index("brick")
    odd_b = brick % 2 == 1
    fields = adjoint.shape[0]

    b_valid = jnp.where(odd_b, brick < bricks - 1, brick > 0)
    b_route = both_ways(far_pairs(bricks))
    f_route = both_ways(far_pairs(levels))
    a_groups = near_pairs(bricks)
    n_groups = near_pairs(levels)
    columns = [
        [b * levels + l for b in pair for l in range(levels)]
        for pair in far_pairs(bricks) + [(bricks - 1, 0)]
    ]

    bf16 = jnp.bfloat16
    whole = ((FIELDS * TILE, LANES), f32)
    state = ((STATE, SIDE, LANES), bf16)
    full = ((STATE + FIXED, SIDE, LANES), bf16)
    state_ends = ((STATE + 4, SIDE, LANES), bf16)
    full_ends = ((STATE + FIXED + 4, SIDE, LANES), bf16)
    strip = (FIELDS, SIDE, LANES)
    corner = (4, SIDE, LANES)
    many = (FIELDS * FIELDS * TILE, LANES)

    flat = lambda values: values.reshape(-1, LANES)
    params = (flat(source), block, precond, flat(couple), flat(solid))
    cells = flat(adjoint)

    def brick_exchange(b_send, a_send):
        b_got = lax.ppermute(b_send, "brick", b_route)
        a_got = lax.all_gather(a_send, "brick", axis_index_groups=a_groups)
        return b_got, a_got

    def level_exchange(f_send, n_send):
        f_got = lax.ppermute(f_send, "level", f_route)
        n_got = lax.all_gather(n_send, "level", axis_index_groups=n_groups)
        return f_got, n_got

    given = (cells,) + params
    cells, *params, b_send, a_send = call(
        first_kernel, [(v.shape, v.dtype) for v in given] + [full, full],
        [whole[0], (TILE, LANES), many, (2 * TILE, LANES)], *given, resident=False,
    )
    b_got, a_got = brick_exchange(b_send, a_send)
    f_send, n_send = call(
        functools.partial(second_kernel, True), [full_ends, full_ends],
        [strip, strip, (SIDE, LANES)], cells, *params, b_got, a_got,
    )
    f_got, n_got = level_exchange(f_send, n_send)
    old = (f_got, n_got, b_got, a_got)
    cells, b_send, a_send = call(
        third_kernel, [whole, state, state],
        [whole[0], whole[0], (TILE, LANES), many, strip, strip, strip, strip, corner],
        cells, *params, *old,
    )
    b_got, a_got = brick_exchange(b_send, a_send)
    f_send, n_send = call(
        functools.partial(second_kernel, False), [state_ends, state_ends],
        [strip, strip, (SIDE, LANES)], cells, *params, b_got, a_got,
    )
    f_got, n_got = level_exchange(f_send, n_send)
    square = ((LANES, LANES), f32)
    smoothed, own, a_row, b_row = call(
        last_kernel, [whole, square, ((FIELDS * OUTER + 2, LANES), f32), square],
        [whole[0], strip, strip, strip, strip, corner, (FIELDS * OUTER * SIDE, LANES),
         (FIELDS * OUTER + 2, LANES), (FIELDS * OUTER + 2, LANES)],
        cells, *params, f_got, n_got, b_got, a_got, *old,
    )
    smoothed = smoothed.reshape(adjoint.shape)
    a_got = lax.all_gather(a_row, "brick", axis_index_groups=a_groups)
    half_x, half_y = HALF, HALF

    nz = adjoint.shape[3]
    zblock = nz // (2 * levels)
    slots = jnp.arange(levels, dtype=jnp.int32)
    inverse = jnp.sum(jnp.where(coarse_owner[None, :] == slots[:, None], slots[None, :], 0), axis=1)
    target = (inverse[:, None] * zblock + jnp.arange(zblock, dtype=jnp.int32)[None, :]).reshape(-1, 1)
    fine = jnp.arange(nz, dtype=jnp.int32)[None, :]
    weights = jnp.where(fine == 2 * target, 0.5, 0.0) + jnp.where(
        (fine == 2 * target + 1) | (fine == 2 * target - 1), 0.25, 0.0
    )

    (send,) = call(
        send_kernel, [square], [square[0]], weights.astype(bf16), own, a_got, b_row
    )
    send = send.reshape(2 * levels, zblock, LANES)
    got = lax.all_to_all(
        send, BOTH, split_axis=0, concat_axis=0, tiled=True, axis_index_groups=columns
    )
    own_got = jnp.where(odd_b, got[:levels], got[levels:])
    edge_got = jnp.where(odd_b, got[levels:], got[:levels])
    rows = fields * (half_x + 2)
    own_got = own_got[..., : rows * half_y].reshape(levels, zblock, fields, half_x + 2, half_y)
    edge_got = edge_got[..., :rows].reshape(levels, zblock, fields, half_x + 2, 1)
    b_at = jnp.where(odd_b, half_y - 1, 0)
    rest = jnp.where((jnp.arange(half_y) == b_at) & b_valid, edge_got, 0.0)
    total = own_got + rest
    up = total[:-1, :, :, -1:]
    down = total[1:, :, :, :1]
    none = jnp.zeros_like(total[:1, :, :, :1])
    up = jnp.concatenate([none, up], 0)
    down = jnp.concatenate([down, none], 0)
    body = total[:, :, :, 1:-1]
    body = jnp.concatenate(
        [body[:, :, :, :1] + up, body[:, :, :, 1:-1], body[:, :, :, -1:] + down], 3
    )
    coarse_rhs = body.transpose(2, 0, 3, 4, 1).reshape(
        fields, levels * half_x, half_y, zblock
    )[None]
    return (smoothed, coarse_rhs)


def solution(mesh):
    placed = (
        P(None, "level", "brick", None),
        P(None, "level", "brick", None),
        P(None, None, "level", "brick", None),
        P(None, None, "level", "brick", None),
        P(None, "level", "brick", None),
        P("level", "brick", None),
        P(),
    )
    return jax.shard_map(
        shards,
        mesh=mesh,
        in_specs=placed,
        out_specs=(P(None, "level", "brick", None), P("level", None, None, "brick", None)),
        check_vma=False,
    )
```

```python
import functools

import jax
import jax.numpy as jnp
from jax import lax
from jax.experimental import pallas as pl
from jax.experimental.pallas import tpu as pltpu
from jax.sharding import PartitionSpec as P


relax_factor = 0.8
BOTH = ("brick", "level")
FIELDS = 5
SIDE = 8
TILE = SIDE * SIDE
LANES = 128
STATE = 4 * FIELDS
FIXED = 4 + FIELDS * FIELDS
HALF = SIDE // 2
OUTER = HALF + 2
f32 = jnp.float32


def far_pairs(count):
    return [(i, i + 1) for i in range(1, count - 1, 2)]


def near_pairs(count):
    return [[i, i + 1] for i in range(0, count, 2)]


def both_ways(pairs):
    return pairs + [(b, a) for a, b in pairs]


def iota(axis):
    return lax.broadcasted_iota(jnp.int32, (SIDE, LANES), axis)


def tile(ref, field, x):
    return ref[pl.ds((field * SIDE + x) * SIDE, SIDE), :]


def y_edge(ref, field, y):
    return ref[pl.ds(field * TILE + y, SIDE, stride=SIDE), :]


def put(ref, index, value):
    high = value.astype(jnp.bfloat16)
    ref[index] = high
    return (value - high.astype(f32)).astype(jnp.bfloat16)


def put_wide(ref, start, count, index, value):
    ref[start + count + index] = put(ref, start + index, value)


def wide(planes, start, count, index):
    return planes(start + index).astype(f32) + planes(start + count + index).astype(f32)


def shifted(value, axis):
    size = value.shape[axis]
    at = iota(axis)
    before = jnp.where(at == 0, 0.0, pltpu.roll(value, 1, axis))
    after = jnp.where(at == size - 1, 0.0, pltpu.roll(value, size - 1, axis))
    return before + after


def defect_tile(s, halo, source, block, couple, x):
    x_low, x_high, y_low, y_high = halo
    here = [tile(s, field, x) for field in range(FIELDS)]
    c0, c1, c2 = (tile(couple, axis, x) for axis in range(3))
    row = iota(0)
    out = []
    for outer in range(FIELDS):
        total = block[0, outer, x].astype(f32) * here[0]
        for inner in range(1, FIELDS):
            total = total + block[inner, outer, x].astype(f32) * here[inner]
        near_y = shifted(here[outer], 0)
        if y_low is not None:
            near_y = near_y + jnp.where(row == 0, y_low(outer, x), 0.0)
            near_y = near_y + jnp.where(row == SIDE - 1, y_high(outer, x), 0.0)
        coupled = c1 * near_y + c2 * shifted(here[outer], 1)
        near_x = None
        if x > 0:
            near_x = tile(s, outer, x - 1)
        elif x_low is not None:
            near_x = x_low(outer)
        other = None
        if x < SIDE - 1:
            other = tile(s, outer, x + 1)
        elif x_high is not None:
            other = x_high(outer)
        both = [v for v in (near_x, other) if v is not None]
        coupled = coupled + c0 * (both[0] if len(both) == 1 else both[0] + both[1])
        out.append(tile(source, outer, x) - (total - coupled))
    return out


def stepped(precond, defect):
    out = []
    for outer in range(FIELDS):
        total = precond(outer, 0) * defect[0]
        for inner in range(1, FIELDS):
            total = total + precond(outer, inner) * defect[inner]
        out.append(total)
    return out


def sweep(s, halo, ins, out):
    for x in range(SIDE):
        defect = defect_tile(s, halo, ins.source, ins.block, ins.couple, x)
        step = stepped(lambda o, i: ins.precond[o, i, x].astype(f32), defect)
        keep = ins.solid[pl.ds(x * SIDE, SIDE), :] == 0
        for field in range(FIELDS):
            value = jnp.where(keep, tile(s, field, x) + relax_factor * step[field], 0.0)
            out[pl.ds((field * SIDE + x) * SIDE, SIDE), :] = value


class Cells:
    def __init__(self, source, block, precond, couple, solid):
        self.source, self.block, self.precond = source, block, precond
        self.couple, self.solid = couple, solid


def y_state(s, ins, odd_b, sends, d, keeps, pf, opens):
    none = (None,) * 4
    for x in range(SIDE):
        defect = defect_tile(s, none, ins.source, ins.block, ins.couple, x)
        for field in range(FIELDS):
            d[pl.ds((field * SIDE + x) * SIDE, SIDE), :] = defect[field]
    for side, send in zip("BA", sends):
        above = odd_b if side == "B" else 1 - odd_b
        y = above * (SIDE - 1)
        p = [[y_edge(pf, o * FIELDS + i, y) for i in range(FIELDS)] for o in range(FIELDS)]
        step = stepped(lambda o, i: p[o][i], [y_edge(d, i, y) for i in range(FIELDS)])
        keep = y_edge(keeps, 0, y) == 0.0
        for field in range(FIELDS):
            edge = y_edge(s, field, y)
            put_wide(send, 0, 2 * FIELDS, field, edge)
            base = jnp.where(keep, edge + relax_factor * step[field], 0.0)
            put_wide(send, 0, 2 * FIELDS, FIELDS + field, base)
        if opens is not None:
            put_wide(send, STATE, 2, 0, y_edge(opens, 1, y))
            put_wide(send, STATE, 2, 1, y_edge(opens, 0, y))
            for o in range(FIELDS):
                for i in range(FIELDS):
                    send[STATE + 4 + o * FIELDS + i] = p[o][i].astype(jnp.bfloat16)


def fill(ins, pf, keeps, opens):
    for x in range(SIDE):
        solid = ins.solid[pl.ds(x * SIDE, SIDE), :]
        keeps[pl.ds(x * SIDE, SIDE), :] = solid.astype(f32)
        if opens is not None:
            for axis in range(2):
                rows = pl.ds((axis * SIDE + x) * SIDE, SIDE)
                opens[rows, :] = jnp.where(solid == 0, tile(ins.couple, axis, x), 0.0)
        for o in range(FIELDS):
            for i in range(FIELDS):
                rows = pl.ds(((o * FIELDS + i) * SIDE + x) * SIDE, SIDE)
                pf[rows, :] = ins.precond[o, i, x].astype(f32)


def first_kernel(
    odd, s_hbm, source_hbm, block_hbm, precond_hbm, couple_hbm, solid_hbm,
    s, source, block, precond, couple, solid, b_send, a_send,
    d, keeps, pf, opens, done,
):
    pairs = (
        (solid_hbm, solid), (couple_hbm, couple), (s_hbm, s),
        (precond_hbm, precond), (source_hbm, source), (block_hbm, block),
    )
    copies = [pltpu.make_async_copy(a, b, done.at[k]) for k, (a, b) in enumerate(pairs)]
    for copy in copies:
        copy.start()
    for copy in copies[:4]:
        copy.wait()
    ins = Cells(source, block, precond, couple, solid)
    fill(ins, pf, keeps, opens)
    for copy in copies[4:]:
        copy.wait()
    y_state(s, ins, odd[1], (b_send, a_send), d, keeps, pf, opens)


def y_halos(odd_b, b_got, a_got, low, high):
    partner = 1 - odd_b
    for field in range(FIELDS):
        a = wide(lambda k: a_got[partner, k], 0, 2 * FIELDS, field)
        b = wide(lambda k: b_got[k], 0, 2 * FIELDS, field)
        is_odd = odd_b == 1
        low[field] = jnp.where(is_odd, a, b)
        high[field] = jnp.where(is_odd, b, a)


def row_of(ref, field, x):
    return jnp.broadcast_to(ref[field, pl.ds(x, 1), :], (SIDE, LANES))


def second_kernel(
    fixed, odd, s, source, block, precond, couple, solid, b_got, a_got, f_send, n_send, low, high, flat
):
    ins = Cells(source, block, precond, couple, solid)
    odd_l, odd_b = odd[0], odd[1]
    is_odd = odd_l == 1
    y_halos(odd_b, b_got, a_got, low, high)
    halo = (None, None, lambda f, x: row_of(low, f, x), lambda f, x: row_of(high, f, x))
    ends = (0, SIDE - 1)
    edges, bases, pairs = [], [], []
    for x in ends:
        defect = defect_tile(s, halo, source, block, couple, x)
        step = stepped(lambda o, i: precond[o, i, x].astype(f32), defect)
        keep = solid[pl.ds(x * SIDE, SIDE), :] == 0
        edge = [tile(s, field, x) for field in range(FIELDS)]
        edges.append(edge)
        bases.append([jnp.where(keep, e + relax_factor * t, 0.0) for e, t in zip(edge, step)])
        pairs.append([jnp.where(keep, tile(couple, axis, x), 0.0) for axis in range(2)])
    for send, low_side in ((f_send, ~is_odd), (n_send, is_odd)):
        for field in range(FIELDS):
            put_wide(send, 0, 2 * FIELDS, field, jnp.where(low_side, edges[0][field], edges[1][field]))
            base = jnp.where(low_side, bases[0][field], bases[1][field])
            put_wide(send, 0, 2 * FIELDS, FIELDS + field, base)
        count = STATE
        if fixed:
            for axis in range(2):
                pair = jnp.where(low_side, pairs[0][axis], pairs[1][axis])
                put_wide(send, STATE, 2, axis, pair)
            for o in range(FIELDS):
                for i in range(FIELDS):
                    at_low = precond[o, i, 0].astype(f32)
                    at_high = precond[o, i, SIDE - 1].astype(f32)
                    value = jnp.where(low_side, at_low, at_high)
                    send[STATE + 4 + o * FIELDS + i] = value.astype(jnp.bfloat16)
            count += FIXED
        x = jnp.where(low_side, 0, SIDE - 1)
        for index, a_side in enumerate((True, False)):
            flat[...] = jnp.zeros((SIDE, LANES), f32)
            for field in range(FIELDS):
                at_low = low[field, pl.ds(x, 1), :]
                at_high = high[field, pl.ds(x, 1), :]
                low_is_it = (odd_b == 1) if a_side else (odd_b == 0)
                flat[pl.ds(field, 1), :] = jnp.where(low_is_it, at_low, at_high)
            put_wide(send, count + 2 * index, 1, 0, flat[...])


def ring_into(odd, s, got, fixed, low, high, x_low, x_high, corners):
    odd_l, odd_b = odd[0], odd[1]
    is_odd_l, is_odd_b = odd_l == 1, odd_b == 1
    row = iota(0)
    tail = STATE + (FIXED if got["fixed"] else 0)
    for k, (name, start) in enumerate((("F", tail), ("F", tail + 2), ("N", tail), ("N", tail + 2))):
        corners[k] = wide(got[name], start, 1, 0)
    rings = {}
    for side in "FNAB":
        planes, kept = got[side], fixed[side]
        normal = wide(kept, STATE, 2, 0)
        missing = []
        if side in "FN":
            above = odd_l if side == "F" else 1 - odd_l
            for field in range(FIELDS):
                inner = jnp.where(above == 1, tile(s, field, SIDE - 1), tile(s, field, 0))
                missing.append(normal * inner)
        else:
            above = odd_b if side == "B" else 1 - odd_b
            tangent = wide(kept, STATE, 2, 1)
            far, near = (0, 2) if side == "A" else (1, 3)
            for field in range(FIELDS):
                inner = y_edge(s, field, above * (SIDE - 1))
                far_row = row_of(corners, far, field)
                near_row = row_of(corners, near, field)
                first = jnp.where(is_odd_l, near_row, far_row)
                final = jnp.where(is_odd_l, far_row, near_row)
                ends = jnp.where(row == 0, first, jnp.where(row == SIDE - 1, final, 0.0))
                missing.append(normal * inner + tangent * ends)
        step = stepped(lambda o, i: kept(STATE + 4 + o * FIELDS + i).astype(f32), missing)
        rings[side] = [
            wide(planes, 0, 2 * FIELDS, FIELDS + field) + relax_factor * step[field]
            for field in range(FIELDS)
        ]
    for field in range(FIELDS):
        f, n, a, b = (rings[side][field] for side in "FNAB")
        x_low[field] = jnp.where(is_odd_l, n, f)
        x_high[field] = jnp.where(is_odd_l, f, n)
        low[field] = jnp.where(is_odd_b, a, b)
        high[field] = jnp.where(is_odd_b, b, a)


def two_sweeps(odd, s, ins, got, fixed, middle, out, halos):
    low, high, x_low, x_high, corners = halos
    odd_l, odd_b = odd[0], odd[1]
    is_odd_l = odd_l == 1
    y_halos(odd_b, *got["y"], low, high)
    for field in range(FIELDS):
        f = wide(got["F"], 0, 2 * FIELDS, field)
        n = wide(got["N"], 0, 2 * FIELDS, field)
        x_low[field] = jnp.where(is_odd_l, n, f)
        x_high[field] = jnp.where(is_odd_l, f, n)
    halo = (
        lambda field: x_low[field],
        lambda field: x_high[field],
        lambda field, x: row_of(low, field, x),
        lambda field, x: row_of(high, field, x),
    )
    sweep(s, halo, ins, middle)
    ring_into(odd, s, got, fixed, low, high, x_low, x_high, corners)
    sweep(middle, halo, ins, out)


def readers(odd, f_got, n_got, b_got, a_got):
    l, b = 1 - odd[0], 1 - odd[1]
    return {
        "F": lambda k: f_got[k],
        "N": lambda k: n_got[l, k],
        "A": lambda k: a_got[b, k],
        "B": lambda k: b_got[k],
    }


def third_kernel(
    odd, s, source, block, precond, couple, solid, f_got, n_got, b_got, a_got,
    out, b_send, a_send,
    middle, d, keeps, pf, low, high, x_low, x_high, corners,
):
    ins = Cells(source, block, precond, couple, solid)
    got = readers(odd, f_got, n_got, b_got, a_got)
    fixed = dict(got)
    got["fixed"], got["y"] = True, (b_got, a_got)
    two_sweeps(odd, s, ins, got, fixed, middle, out, (low, high, x_low, x_high, corners))
    fill(ins, pf, keeps, None)
    y_state(out, ins, odd[1], (b_send, a_send), d, keeps, pf, None)


def last_kernel(
    odd, s, source, block, precond, couple, solid, f_got, n_got, b_got, a_got, f_old, n_old, b_old, a_old,
    out, own, a_row, b_row,
    middle, low, high, x_low, x_high, corners, grid, below, above,
):
    ins = Cells(source, block, precond, couple, solid)
    got = readers(odd, f_got, n_got, b_got, a_got)
    fixed = readers(odd, f_old, n_old, b_old, a_old)
    got["fixed"], got["y"] = False, (b_got, a_got)
    two_sweeps(odd, s, ins, got, fixed, middle, out, (low, high, x_low, x_high, corners))
    odd_l, odd_b = odd[0], odd[1]
    is_odd_l, is_odd_b = odd_l == 1, odd_b == 1
    none = (None,) * 4
    for x in range(SIDE):
        defect = defect_tile(out, none, source, block, couple, x)
        keep = solid[pl.ds(x * SIDE, SIDE), :] == 0
        for field in range(FIELDS):
            rows = pl.ds((field * SIDE + x) * SIDE, SIDE)
            middle[rows, :] = jnp.where(keep, defect[field], 0.0)
    normal = {side: wide(fixed[side], STATE, 2, 0) for side in "FNAB"}
    row = iota(0)
    for field in range(FIELDS):
        y_at_a, y_at_b = (1 - odd_b) * (SIDE - 1), odd_b * (SIDE - 1)
        a = normal["A"] * y_edge(out, field, y_at_a)
        b = normal["B"] * y_edge(out, field, y_at_b)
        for ref, beyond in ((below, jnp.where(is_odd_b, a, b)), (above, jnp.where(is_odd_b, b, a))):
            even = 0.5 * beyond + 0.25 * shifted(beyond, 0)
            ref[pl.ds(field, 1), :] = jnp.zeros((1, LANES), f32)
            for k in range(HALF):
                ref[pl.ds((1 + k) * FIELDS + field, 1), :] = even[2 * k : 2 * k + 1]
            ref[pl.ds((OUTER - 1) * FIELDS + field, 1), :] = 0.25 * beyond[SIDE - 1 :]
    for field in range(FIELDS):
        first, final = tile(out, field, 0), tile(out, field, SIDE - 1)
        f = normal["F"] * jnp.where(is_odd_l, final, first)
        n = normal["N"] * jnp.where(is_odd_l, first, final)
        fine = [tile(middle, field, x) for x in range(SIDE)]
        before, after = jnp.where(is_odd_l, n, f), jnp.where(is_odd_l, f, n)
        coarse = [0.25 * before]
        for k in range(HALF):
            earlier = fine[2 * k - 1] if k else before
            coarse.append(0.5 * fine[2 * k] + 0.25 * (fine[2 * k + 1] + earlier))
        coarse.append(0.5 * after + 0.25 * fine[SIDE - 1])
        for k in range(OUTER):
            value = coarse[k]
            index = k * FIELDS + field
            under = below[pl.ds(index, 1), :]
            even = 0.5 * value + 0.25 * shifted(value, 0)
            even = even + jnp.where(row == 0, jnp.broadcast_to(0.25 * under, (SIDE, LANES)), 0.0)
            grid[pl.ds(index * SIDE, SIDE), :] = even
            over = 0.5 * above[pl.ds(index, 1), :] + 0.25 * value[SIDE - 1 :]
            a_row[pl.ds(index, 1), :] = jnp.where(is_odd_b, 0.25 * under, over)
            b_row[pl.ds(index, 1), :] = jnp.where(is_odd_b, over, 0.25 * under)
    count = FIELDS * OUTER
    own[pl.ds(0, count * HALF), :] = grid[pl.ds(0, count * HALF, stride=2), :]
    own[pl.ds(count * HALF, LANES - count * HALF), :] = jnp.zeros((LANES - count * HALF, LANES), f32)
    b_row[pl.ds(count, 2), :] = jnp.zeros((2, LANES), f32)
    a_row[pl.ds(count, 2), :] = jnp.zeros((2, LANES), f32)


def send_kernel(odd, weights, own, a_got, b_row, send, rows, edge):
    odd_b = odd[1]
    count = FIELDS * OUTER
    rows[...] = own[...]
    at = pl.ds((1 - odd_b) * (HALF - 1), count, stride=HALF)
    rows[at, :] = rows[at, :] + a_got[1 - odd_b, pl.ds(0, count), :]

    edge[...] = jnp.zeros_like(edge)
    edge[pl.ds((1 - odd_b) * (HALF - 1), count, stride=HALF), :] = b_row[pl.ds(0, count), :]
    values = jnp.concatenate([rows[...], edge[...]], 0)
    size = weights.shape[0]
    total = jnp.zeros((size, 2 * LANES), f32)
    for _ in range(3):
        part = values.astype(jnp.bfloat16)
        values = values - part.astype(f32)
        total = total + lax.dot_general(
            weights[...], part, (((1,), (1,)), ((), ())), preferred_element_type=f32
        )
    send[pl.ds(pl.multiple_of((1 - odd_b) * size, size), size), :] = total[:, :LANES]
    send[pl.ds(pl.multiple_of(odd_b * size, size), size), :] = total[:, LANES:]


def final_kernel(bricks, odd, got, out, turned):
    odd_b = odd[1]
    brick = lax.axis_index("brick")
    size = got.shape[0] // 2
    own = got[pl.ds(pl.multiple_of((1 - odd_b) * size, size), size), :]
    edge = got[pl.ds(pl.multiple_of(odd_b * size, size), size), :]
    valid = (brick > 0) & (brick < bricks - 1)
    total = own + jnp.where(valid, edge, 0.0)
    turned[...] = jnp.concatenate([total, jnp.zeros((LANES - size, LANES), f32)], 0).T
    cells = FIELDS * HALF
    rows = 24
    lane = lax.broadcasted_iota(jnp.int32, (rows, LANES), 1) % HALF
    blocks = [turned[pl.ds(cells * x, rows), :] for x in range(OUTER)]
    for k in range(HALF):
        total = jnp.zeros((rows, LANES), f32)
        for index, block in enumerate(blocks):
            x = index - 1
            moved = block if x == k else pltpu.roll(block, (x - k) % LANES, 1)
            total = total + jnp.where(lane == x % HALF, moved, 0.0)
        out[pl.ds(k, cells, stride=HALF), :] = total[:cells, : out.shape[1]]


def call(kernel, outs, scratch, *args, resident=True):
    space = pltpu.VMEM if resident else pltpu.HBM
    args = [pltpu.with_memory_space_constraint(arg, space) for arg in args]
    copies = [] if resident else [pltpu.SemaphoreType.DMA((len(args),))]

    def body(*refs):
        kernel(tuple(lax.rem(lax.axis_index(axis), 2) for axis in ("level", "brick")), *refs)

    return pl.pallas_call(
        body,
        out_shape=[pltpu.VMEM(shape, dtype) for shape, dtype in outs],
        in_specs=[pl.BlockSpec(memory_space=space)] * len(args),
        out_specs=[pl.BlockSpec(memory_space=pltpu.VMEM)] * len(outs),
        scratch_shapes=[pltpu.VMEM(shape, f32) for shape in scratch] + copies,
        compiler_params=pltpu.CompilerParams(vmem_limit_bytes=16 * 1024 * 1024),
    )(*args)


def shards(adjoint, source, block, precond, couple, solid, coarse_owner):
    levels = lax.axis_size("level")
    bricks = lax.axis_size("brick")
    b_route = both_ways(far_pairs(bricks))
    f_route = both_ways(far_pairs(levels))
    a_groups = near_pairs(bricks)
    n_groups = near_pairs(levels)
    columns = [
        [b * levels + l for b in pair for l in range(levels)]
        for pair in far_pairs(bricks) + [(bricks - 1, 0)]
    ]

    bf16 = jnp.bfloat16
    whole = ((FIELDS * TILE, LANES), f32)
    state = ((STATE, SIDE, LANES), bf16)
    full = ((STATE + FIXED, SIDE, LANES), bf16)
    state_ends = ((STATE + 4, SIDE, LANES), bf16)
    full_ends = ((STATE + FIXED + 4, SIDE, LANES), bf16)
    strip = (FIELDS, SIDE, LANES)
    corner = (4, SIDE, LANES)
    many = (FIELDS * FIELDS * TILE, LANES)

    flat = lambda values: values.reshape(-1, LANES)
    params = (flat(source), block, precond, flat(couple), flat(solid))
    cells = flat(adjoint)

    def brick_exchange(b_send, a_send):
        b_got = lax.ppermute(b_send, "brick", b_route)
        a_got = lax.all_gather(a_send, "brick", axis_index_groups=a_groups)
        return b_got, a_got

    def level_exchange(f_send, n_send):
        f_got = lax.ppermute(f_send, "level", f_route)
        n_got = lax.all_gather(n_send, "level", axis_index_groups=n_groups)
        return f_got, n_got

    given = (cells,) + params
    cells, *params, b_send, a_send = call(
        first_kernel, [(v.shape, v.dtype) for v in given] + [full, full],
        [whole[0], (TILE, LANES), many, (2 * TILE, LANES)], *given, resident=False,
    )
    b_got, a_got = brick_exchange(b_send, a_send)
    f_send, n_send = call(
        functools.partial(second_kernel, True), [full_ends, full_ends],
        [strip, strip, (SIDE, LANES)], cells, *params, b_got, a_got,
    )
    f_got, n_got = level_exchange(f_send, n_send)
    old = (f_got, n_got, b_got, a_got)
    cells, b_send, a_send = call(
        third_kernel, [whole, state, state],
        [whole[0], whole[0], (TILE, LANES), many, strip, strip, strip, strip, corner],
        cells, *params, *old,
    )
    b_got, a_got = brick_exchange(b_send, a_send)
    f_send, n_send = call(
        functools.partial(second_kernel, False), [state_ends, state_ends],
        [strip, strip, (SIDE, LANES)], cells, *params, b_got, a_got,
    )
    f_got, n_got = level_exchange(f_send, n_send)
    square = ((LANES, LANES), f32)
    edge_rows = ((FIELDS * OUTER + 2, LANES), f32)
    smoothed, own, a_row, b_row = call(
        last_kernel, [whole, square, edge_rows, edge_rows],
        [whole[0], strip, strip, strip, strip, corner, (FIELDS * OUTER * SIDE, LANES),
         (FIELDS * OUTER + 2, LANES), (FIELDS * OUTER + 2, LANES)],
        cells, *params, f_got, n_got, b_got, a_got, *old,
    )
    smoothed = smoothed.reshape(adjoint.shape)
    a_got = lax.all_gather(a_row, "brick", axis_index_groups=a_groups)

    nz = adjoint.shape[3]
    zblock = nz // (2 * levels)
    slots = jnp.arange(levels, dtype=jnp.int32)
    inverse = jnp.sum(jnp.where(coarse_owner[None, :] == slots[:, None], slots[None, :], 0), axis=1)
    target = (inverse[:, None] * zblock + jnp.arange(zblock, dtype=jnp.int32)[None, :]).reshape(-1, 1)
    fine = jnp.arange(nz, dtype=jnp.int32)[None, :]
    weights = jnp.where(fine == 2 * target, 0.5, 0.0) + jnp.where(
        (fine == 2 * target + 1) | (fine == 2 * target - 1), 0.25, 0.0
    )

    (send,) = call(
        send_kernel, [square], [square[0], square[0]], weights.astype(bf16), own, a_got, b_row
    )
    send = send.reshape(2 * levels, zblock, LANES)
    got = lax.all_to_all(
        send, BOTH, split_axis=0, concat_axis=0, tiled=True, axis_index_groups=columns
    )
    (coarse_rhs,) = call(
        functools.partial(final_kernel, bricks), [((FIELDS * HALF * zblock, levels * HALF), f32)],
        [square[0]], got.reshape(LANES, LANES),
    )
    coarse_rhs = coarse_rhs.reshape(FIELDS, HALF, zblock, levels * HALF)
    coarse_rhs = coarse_rhs.transpose(0, 3, 1, 2)[None]
    return (smoothed, coarse_rhs)


def solution(mesh):
    placed = (
        P(None, "level", "brick", None),
        P(None, "level", "brick", None),
        P(None, None, "level", "brick", None),
        P(None, None, "level", "brick", None),
        P(None, "level", "brick", None),
        P("level", "brick", None),
        P(),
    )
    return jax.shard_map(
        shards,
        mesh=mesh,
        in_specs=placed,
        out_specs=(P(None, "level", "brick", None), P("level", None, None, "brick", None)),
        check_vma=False,
    )
```

```python
import functools

import jax
import jax.numpy as jnp
from jax import lax
from jax.experimental import pallas as pl
from jax.experimental.pallas import tpu as pltpu
from jax.sharding import PartitionSpec as P


relax_factor = 0.8
BOTH = ("brick", "level")
FIELDS = 5
SIDE = 8
TILE = SIDE * SIDE
LANES = 128
STATE = 4 * FIELDS
FIXED = 4 + FIELDS * FIELDS
HALF = SIDE // 2
OUTER = HALF + 2
f32 = jnp.float32


def far_pairs(count):
    return [(i, i + 1) for i in range(1, count - 1, 2)]


def near_pairs(count):
    return [[i, i + 1] for i in range(0, count, 2)]


def both_ways(pairs):
    return pairs + [(b, a) for a, b in pairs]


def iota(axis):
    return lax.broadcasted_iota(jnp.int32, (SIDE, LANES), axis)


def tile(ref, field, x):
    return ref[pl.ds((field * SIDE + x) * SIDE, SIDE), :]


def y_edge(ref, field, y):
    return ref[pl.ds(field * TILE + y, SIDE, stride=SIDE), :]


def put(ref, index, value):
    high = value.astype(jnp.bfloat16)
    ref[index] = high
    return (value - high.astype(f32)).astype(jnp.bfloat16)


def put_wide(ref, start, count, index, value):
    ref[start + count + index] = put(ref, start + index, value)


def wide(planes, start, count, index):
    return planes(start + index).astype(f32) + planes(start + count + index).astype(f32)


def shifted(value, axis):
    size = value.shape[axis]
    at = iota(axis)
    before = jnp.where(at == 0, 0.0, pltpu.roll(value, 1, axis))
    after = jnp.where(at == size - 1, 0.0, pltpu.roll(value, size - 1, axis))
    return before + after


def defect_tile(s, halo, source, block, couple, x):
    x_low, x_high, y_low, y_high = halo
    here = [tile(s, field, x) for field in range(FIELDS)]
    c0, c1, c2 = (tile(couple, axis, x) for axis in range(3))
    row = iota(0)
    out = []
    for outer in range(FIELDS):
        total = block[0, outer, x].astype(f32) * here[0]
        for inner in range(1, FIELDS):
            total = total + block[inner, outer, x].astype(f32) * here[inner]
        near_y = shifted(here[outer], 0)
        if y_low is not None:
            near_y = near_y + jnp.where(row == 0, y_low(outer, x), 0.0)
            near_y = near_y + jnp.where(row == SIDE - 1, y_high(outer, x), 0.0)
        coupled = c1 * near_y + c2 * shifted(here[outer], 1)
        near_x = None
        if x > 0:
            near_x = tile(s, outer, x - 1)
        elif x_low is not None:
            near_x = x_low(outer)
        other = None
        if x < SIDE - 1:
            other = tile(s, outer, x + 1)
        elif x_high is not None:
            other = x_high(outer)
        both = [v for v in (near_x, other) if v is not None]
        coupled = coupled + c0 * (both[0] if len(both) == 1 else both[0] + both[1])
        out.append(tile(source, outer, x) - (total - coupled))
    return out


def stepped(precond, defect):
    out = []
    for outer in range(FIELDS):
        total = precond(outer, 0) * defect[0]
        for inner in range(1, FIELDS):
            total = total + precond(outer, inner) * defect[inner]
        out.append(total)
    return out


def sweep(s, halo, ins, out):
    for x in range(SIDE):
        defect = defect_tile(s, halo, ins.source, ins.block, ins.couple, x)
        step = stepped(lambda o, i: ins.precond[o, i, x].astype(f32), defect)
        keep = ins.solid[pl.ds(x * SIDE, SIDE), :] == 0
        for field in range(FIELDS):
            value = jnp.where(keep, tile(s, field, x) + relax_factor * step[field], 0.0)
            out[pl.ds((field * SIDE + x) * SIDE, SIDE), :] = value


class Cells:
    def __init__(self, source, block, precond, couple, solid):
        self.source, self.block, self.precond = source, block, precond
        self.couple, self.solid = couple, solid


def y_state(s, ins, odd_b, sends, d, keeps, pf, opens):
    none = (None,) * 4
    for x in range(SIDE):
        defect = defect_tile(s, none, ins.source, ins.block, ins.couple, x)
        for field in range(FIELDS):
            d[pl.ds((field * SIDE + x) * SIDE, SIDE), :] = defect[field]
    for side, send in zip("BA", sends):
        above = odd_b if side == "B" else 1 - odd_b
        y = above * (SIDE - 1)
        p = [[y_edge(pf, o * FIELDS + i, y) for i in range(FIELDS)] for o in range(FIELDS)]
        step = stepped(lambda o, i: p[o][i], [y_edge(d, i, y) for i in range(FIELDS)])
        keep = y_edge(keeps, 0, y) == 0.0
        for field in range(FIELDS):
            edge = y_edge(s, field, y)
            put_wide(send, 0, 2 * FIELDS, field, edge)
            base = jnp.where(keep, edge + relax_factor * step[field], 0.0)
            put_wide(send, 0, 2 * FIELDS, FIELDS + field, base)
        if opens is not None:
            put_wide(send, STATE, 2, 0, y_edge(opens, 1, y))
            put_wide(send, STATE, 2, 1, y_edge(opens, 0, y))
            for o in range(FIELDS):
                for i in range(FIELDS):
                    send[STATE + 4 + o * FIELDS + i] = p[o][i].astype(jnp.bfloat16)


def fill(ins, pf, keeps, opens):
    for x in range(SIDE):
        solid = ins.solid[pl.ds(x * SIDE, SIDE), :]
        keeps[pl.ds(x * SIDE, SIDE), :] = solid.astype(f32)
        if opens is not None:
            for axis in range(2):
                rows = pl.ds((axis * SIDE + x) * SIDE, SIDE)
                opens[rows, :] = jnp.where(solid == 0, tile(ins.couple, axis, x), 0.0)
        for o in range(FIELDS):
            for i in range(FIELDS):
                rows = pl.ds(((o * FIELDS + i) * SIDE + x) * SIDE, SIDE)
                pf[rows, :] = ins.precond[o, i, x].astype(f32)


def first_kernel(
    odd, s_hbm, source_hbm, block_hbm, precond_hbm, couple_hbm, solid_hbm,
    s, source, block, precond, couple, solid, b_send, a_send,
    d, keeps, pf, opens, done,
):
    pairs = (
        (solid_hbm, solid), (couple_hbm, couple), (s_hbm, s),
        (precond_hbm, precond), (source_hbm, source), (block_hbm, block),
    )
    copies = [pltpu.make_async_copy(a, b, done.at[k]) for k, (a, b) in enumerate(pairs)]
    for copy in copies:
        copy.start()
    for copy in copies[:4]:
        copy.wait()
    ins = Cells(source, block, precond, couple, solid)
    fill(ins, pf, keeps, opens)
    for copy in copies[4:]:
        copy.wait()
    y_state(s, ins, odd[1], (b_send, a_send), d, keeps, pf, opens)


def y_halos(odd_b, b_got, a_got, low, high):
    partner = 1 - odd_b
    for field in range(FIELDS):
        a = wide(lambda k: a_got[partner, k], 0, 2 * FIELDS, field)
        b = wide(lambda k: b_got[k], 0, 2 * FIELDS, field)
        is_odd = odd_b == 1
        low[field] = jnp.where(is_odd, a, b)
        high[field] = jnp.where(is_odd, b, a)


def row_of(ref, field, x):
    return jnp.broadcast_to(ref[field, pl.ds(x, 1), :], (SIDE, LANES))


def second_kernel(
    fixed, odd, s, source, block, precond, couple, solid, b_got, a_got, f_send, n_send, low, high, flat
):
    ins = Cells(source, block, precond, couple, solid)
    odd_l, odd_b = odd[0], odd[1]
    is_odd = odd_l == 1
    y_halos(odd_b, b_got, a_got, low, high)
    halo = (None, None, lambda f, x: row_of(low, f, x), lambda f, x: row_of(high, f, x))
    ends = (0, SIDE - 1)
    edges, bases, pairs = [], [], []
    for x in ends:
        defect = defect_tile(s, halo, source, block, couple, x)
        step = stepped(lambda o, i: precond[o, i, x].astype(f32), defect)
        keep = solid[pl.ds(x * SIDE, SIDE), :] == 0
        edge = [tile(s, field, x) for field in range(FIELDS)]
        edges.append(edge)
        bases.append([jnp.where(keep, e + relax_factor * t, 0.0) for e, t in zip(edge, step)])
        pairs.append([jnp.where(keep, tile(couple, axis, x), 0.0) for axis in range(2)])
    for send, low_side in ((f_send, ~is_odd), (n_send, is_odd)):
        for field in range(FIELDS):
            put_wide(send, 0, 2 * FIELDS, field, jnp.where(low_side, edges[0][field], edges[1][field]))
            base = jnp.where(low_side, bases[0][field], bases[1][field])
            put_wide(send, 0, 2 * FIELDS, FIELDS + field, base)
        count = STATE
        if fixed:
            for axis in range(2):
                pair = jnp.where(low_side, pairs[0][axis], pairs[1][axis])
                put_wide(send, STATE, 2, axis, pair)
            for o in range(FIELDS):
                for i in range(FIELDS):
                    at_low = precond[o, i, 0].astype(f32)
                    at_high = precond[o, i, SIDE - 1].astype(f32)
                    value = jnp.where(low_side, at_low, at_high)
                    send[STATE + 4 + o * FIELDS + i] = value.astype(jnp.bfloat16)
            count += FIXED
        x = jnp.where(low_side, 0, SIDE - 1)
        for index, a_side in enumerate((True, False)):
            flat[...] = jnp.zeros((SIDE, LANES), f32)
            for field in range(FIELDS):
                at_low = low[field, pl.ds(x, 1), :]
                at_high = high[field, pl.ds(x, 1), :]
                low_is_it = (odd_b == 1) if a_side else (odd_b == 0)
                flat[pl.ds(field, 1), :] = jnp.where(low_is_it, at_low, at_high)
            put_wide(send, count + 2 * index, 1, 0, flat[...])


def ring_into(odd, s, got, fixed, low, high, x_low, x_high, corners):
    odd_l, odd_b = odd[0], odd[1]
    is_odd_l, is_odd_b = odd_l == 1, odd_b == 1
    row = iota(0)
    tail = STATE + (FIXED if got["fixed"] else 0)
    for k, (name, start) in enumerate((("F", tail), ("F", tail + 2), ("N", tail), ("N", tail + 2))):
        corners[k] = wide(got[name], start, 1, 0)
    rings = {}
    for side in "FNAB":
        planes, kept = got[side], fixed[side]
        normal = wide(kept, STATE, 2, 0)
        missing = []
        if side in "FN":
            above = odd_l if side == "F" else 1 - odd_l
            for field in range(FIELDS):
                inner = jnp.where(above == 1, tile(s, field, SIDE - 1), tile(s, field, 0))
                missing.append(normal * inner)
        else:
            above = odd_b if side == "B" else 1 - odd_b
            tangent = wide(kept, STATE, 2, 1)
            far, near = (0, 2) if side == "A" else (1, 3)
            for field in range(FIELDS):
                inner = y_edge(s, field, above * (SIDE - 1))
                far_row = row_of(corners, far, field)
                near_row = row_of(corners, near, field)
                first = jnp.where(is_odd_l, near_row, far_row)
                final = jnp.where(is_odd_l, far_row, near_row)
                ends = jnp.where(row == 0, first, jnp.where(row == SIDE - 1, final, 0.0))
                missing.append(normal * inner + tangent * ends)
        step = stepped(lambda o, i: kept(STATE + 4 + o * FIELDS + i).astype(f32), missing)
        rings[side] = [
            wide(planes, 0, 2 * FIELDS, FIELDS + field) + relax_factor * step[field]
            for field in range(FIELDS)
        ]
    for field in range(FIELDS):
        f, n, a, b = (rings[side][field] for side in "FNAB")
        x_low[field] = jnp.where(is_odd_l, n, f)
        x_high[field] = jnp.where(is_odd_l, f, n)
        low[field] = jnp.where(is_odd_b, a, b)
        high[field] = jnp.where(is_odd_b, b, a)


def two_sweeps(odd, s, ins, got, fixed, middle, out, halos):
    low, high, x_low, x_high, corners = halos
    odd_l, odd_b = odd[0], odd[1]
    is_odd_l = odd_l == 1
    y_halos(odd_b, *got["y"], low, high)
    for field in range(FIELDS):
        f = wide(got["F"], 0, 2 * FIELDS, field)
        n = wide(got["N"], 0, 2 * FIELDS, field)
        x_low[field] = jnp.where(is_odd_l, n, f)
        x_high[field] = jnp.where(is_odd_l, f, n)
    halo = (
        lambda field: x_low[field],
        lambda field: x_high[field],
        lambda field, x: row_of(low, field, x),
        lambda field, x: row_of(high, field, x),
    )
    sweep(s, halo, ins, middle)
    ring_into(odd, s, got, fixed, low, high, x_low, x_high, corners)
    sweep(middle, halo, ins, out)


def readers(odd, f_got, n_got, b_got, a_got):
    l, b = 1 - odd[0], 1 - odd[1]
    return {
        "F": lambda k: f_got[k],
        "N": lambda k: n_got[l, k],
        "A": lambda k: a_got[b, k],
        "B": lambda k: b_got[k],
    }


def third_kernel(
    odd, s, source, block, precond, couple, solid, f_got, n_got, b_got, a_got,
    out, b_send, a_send,
    middle, d, keeps, pf, low, high, x_low, x_high, corners,
):
    ins = Cells(source, block, precond, couple, solid)
    got = readers(odd, f_got, n_got, b_got, a_got)
    fixed = dict(got)
    got["fixed"], got["y"] = True, (b_got, a_got)
    two_sweeps(odd, s, ins, got, fixed, middle, out, (low, high, x_low, x_high, corners))
    fill(ins, pf, keeps, None)
    y_state(out, ins, odd[1], (b_send, a_send), d, keeps, pf, None)


def last_kernel(
    odd, s, source, block, precond, couple, solid, f_got, n_got, b_got, a_got, f_old, n_old, b_old, a_old,
    weights, out, own, to_a, to_b,
    middle, low, high, x_low, x_high, corners, grid, below, above, a_row, b_row, stacked,
):
    ins = Cells(source, block, precond, couple, solid)
    got = readers(odd, f_got, n_got, b_got, a_got)
    fixed = readers(odd, f_old, n_old, b_old, a_old)
    got["fixed"], got["y"] = False, (b_got, a_got)
    two_sweeps(odd, s, ins, got, fixed, middle, out, (low, high, x_low, x_high, corners))
    odd_l, odd_b = odd[0], odd[1]
    is_odd_l, is_odd_b = odd_l == 1, odd_b == 1
    none = (None,) * 4
    for x in range(SIDE):
        defect = defect_tile(out, none, source, block, couple, x)
        keep = solid[pl.ds(x * SIDE, SIDE), :] == 0
        for field in range(FIELDS):
            rows = pl.ds((field * SIDE + x) * SIDE, SIDE)
            middle[rows, :] = jnp.where(keep, defect[field], 0.0)
    normal = {side: wide(fixed[side], STATE, 2, 0) for side in "FNAB"}
    row = iota(0)
    for field in range(FIELDS):
        y_at_a, y_at_b = (1 - odd_b) * (SIDE - 1), odd_b * (SIDE - 1)
        a = normal["A"] * y_edge(out, field, y_at_a)
        b = normal["B"] * y_edge(out, field, y_at_b)
        for ref, beyond in ((below, jnp.where(is_odd_b, a, b)), (above, jnp.where(is_odd_b, b, a))):
            even = 0.5 * beyond + 0.25 * shifted(beyond, 0)
            ref[pl.ds(field, 1), :] = jnp.zeros((1, LANES), f32)
            for k in range(HALF):
                ref[pl.ds((1 + k) * FIELDS + field, 1), :] = even[2 * k : 2 * k + 1]
            ref[pl.ds((OUTER - 1) * FIELDS + field, 1), :] = 0.25 * beyond[SIDE - 1 :]
    for field in range(FIELDS):
        first, final = tile(out, field, 0), tile(out, field, SIDE - 1)
        f = normal["F"] * jnp.where(is_odd_l, final, first)
        n = normal["N"] * jnp.where(is_odd_l, first, final)
        fine = [tile(middle, field, x) for x in range(SIDE)]
        before, after = jnp.where(is_odd_l, n, f), jnp.where(is_odd_l, f, n)
        coarse = [0.25 * before]
        for k in range(HALF):
            earlier = fine[2 * k - 1] if k else before
            coarse.append(0.5 * fine[2 * k] + 0.25 * (fine[2 * k + 1] + earlier))
        coarse.append(0.5 * after + 0.25 * fine[SIDE - 1])
        for k in range(OUTER):
            value = coarse[k]
            index = k * FIELDS + field
            under = below[pl.ds(index, 1), :]
            even = 0.5 * value + 0.25 * shifted(value, 0)
            even = even + jnp.where(row == 0, jnp.broadcast_to(0.25 * under, (SIDE, LANES)), 0.0)
            grid[pl.ds(index * SIDE, SIDE), :] = even
            over = 0.5 * above[pl.ds(index, 1), :] + 0.25 * value[SIDE - 1 :]
            a_row[pl.ds(index, 1), :] = jnp.where(is_odd_b, 0.25 * under, over)
            b_row[pl.ds(index, 1), :] = jnp.where(is_odd_b, over, 0.25 * under)
    count = FIELDS * OUTER
    stacked[...] = jnp.zeros_like(stacked)
    stacked[pl.ds(0, count * HALF), :] = grid[pl.ds(0, count * HALF, stride=2), :]
    for start, at, ref in ((LANES, odd_b, a_row), (2 * LANES, 1 - odd_b, b_row)):
        stacked[pl.ds(start + at * (HALF - 1), count, stride=HALF), :] = ref[pl.ds(0, count), :]
    values = stacked[...]
    total = jnp.zeros((weights.shape[0], 3 * LANES), f32)
    for _ in range(3):
        part = values.astype(jnp.bfloat16)
        values = values - part.astype(f32)
        total = total + lax.dot_general(
            weights[...], part, (((1,), (1,)), ((), ())), preferred_element_type=f32
        )
    own[...] = total[:, :LANES]
    to_a[...] = total[:, LANES : 2 * LANES]
    to_b[...] = total[:, 2 * LANES :]


def send_kernel(odd, own, a_got, to_b, send):
    odd_b = odd[1]
    size = own.shape[0]
    send[pl.ds(pl.multiple_of((1 - odd_b) * size, size), size), :] = own[...] + a_got[1 - odd_b]
    send[pl.ds(pl.multiple_of(odd_b * size, size), size), :] = to_b[...]


def final_kernel(bricks, odd, got, out, turned):
    odd_b = odd[1]
    brick = lax.axis_index("brick")
    size = got.shape[0] // 2
    own = got[pl.ds(pl.multiple_of((1 - odd_b) * size, size), size), :]
    edge = got[pl.ds(pl.multiple_of(odd_b * size, size), size), :]
    valid = (brick > 0) & (brick < bricks - 1)
    total = own + jnp.where(valid, edge, 0.0)
    turned[...] = jnp.concatenate([total, jnp.zeros((LANES - size, LANES), f32)], 0).T
    cells = FIELDS * HALF
    rows = 24
    lane = lax.broadcasted_iota(jnp.int32, (rows, LANES), 1) % HALF
    blocks = [turned[pl.ds(cells * x, rows), :] for x in range(OUTER)]
    for k in range(HALF):
        total = jnp.zeros((rows, LANES), f32)
        for index, block in enumerate(blocks):
            x = index - 1
            moved = block if x == k else pltpu.roll(block, (x - k) % LANES, 1)
            total = total + jnp.where(lane == x % HALF, moved, 0.0)
        out[pl.ds(k, cells, stride=HALF), :] = total[:cells, : out.shape[1]]


def call(kernel, outs, scratch, *args, resident=True):
    space = pltpu.VMEM if resident else pltpu.HBM
    args = [pltpu.with_memory_space_constraint(arg, space) for arg in args]
    copies = [] if resident else [pltpu.SemaphoreType.DMA((len(args),))]

    def body(*refs):
        kernel(tuple(lax.rem(lax.axis_index(axis), 2) for axis in ("level", "brick")), *refs)

    return pl.pallas_call(
        body,
        out_shape=[pltpu.VMEM(shape, dtype) for shape, dtype in outs],
        in_specs=[pl.BlockSpec(memory_space=space)] * len(args),
        out_specs=[pl.BlockSpec(memory_space=pltpu.VMEM)] * len(outs),
        scratch_shapes=[pltpu.VMEM(shape, f32) for shape in scratch] + copies,
        compiler_params=pltpu.CompilerParams(vmem_limit_bytes=16 * 1024 * 1024),
    )(*args)


def shards(adjoint, source, block, precond, couple, solid, coarse_owner):
    levels = lax.axis_size("level")
    bricks = lax.axis_size("brick")
    b_route = both_ways(far_pairs(bricks))
    f_route = both_ways(far_pairs(levels))
    a_groups = near_pairs(bricks)
    n_groups = near_pairs(levels)
    columns = [
        [b * levels + l for b in pair for l in range(levels)]
        for pair in far_pairs(bricks) + [(bricks - 1, 0)]
    ]

    bf16 = jnp.bfloat16
    whole = ((FIELDS * TILE, LANES), f32)
    state = ((STATE, SIDE, LANES), bf16)
    full = ((STATE + FIXED, SIDE, LANES), bf16)
    state_ends = ((STATE + 4, SIDE, LANES), bf16)
    full_ends = ((STATE + FIXED + 4, SIDE, LANES), bf16)
    strip = (FIELDS, SIDE, LANES)
    corner = (4, SIDE, LANES)
    many = (FIELDS * FIELDS * TILE, LANES)

    flat = lambda values: values.reshape(-1, LANES)
    params = (flat(source), block, precond, flat(couple), flat(solid))
    cells = flat(adjoint)

    def brick_exchange(b_send, a_send):
        b_got = lax.ppermute(b_send, "brick", b_route)
        a_got = lax.all_gather(a_send, "brick", axis_index_groups=a_groups)
        return b_got, a_got

    def level_exchange(f_send, n_send):
        f_got = lax.ppermute(f_send, "level", f_route)
        n_got = lax.all_gather(n_send, "level", axis_index_groups=n_groups)
        return f_got, n_got

    given = (cells,) + params
    cells, *params, b_send, a_send = call(
        first_kernel, [(v.shape, v.dtype) for v in given] + [full, full],
        [whole[0], (TILE, LANES), many, (2 * TILE, LANES)], *given, resident=False,
    )
    b_got, a_got = brick_exchange(b_send, a_send)
    f_send, n_send = call(
        functools.partial(second_kernel, True), [full_ends, full_ends],
        [strip, strip, (SIDE, LANES)], cells, *params, b_got, a_got,
    )
    f_got, n_got = level_exchange(f_send, n_send)
    old = (f_got, n_got, b_got, a_got)
    cells, b_send, a_send = call(
        third_kernel, [whole, state, state],
        [whole[0], whole[0], (TILE, LANES), many, strip, strip, strip, strip, corner],
        cells, *params, *old,
    )
    b_got, a_got = brick_exchange(b_send, a_send)
    f_send, n_send = call(
        functools.partial(second_kernel, False), [state_ends, state_ends],
        [strip, strip, (SIDE, LANES)], cells, *params, b_got, a_got,
    )
    f_got, n_got = level_exchange(f_send, n_send)
    nz = adjoint.shape[3]
    zblock = nz // (2 * levels)
    slots = jnp.arange(levels, dtype=jnp.int32)
    inverse = jnp.sum(jnp.where(coarse_owner[None, :] == slots[:, None], slots[None, :], 0), axis=1)
    target = (inverse[:, None] * zblock + jnp.arange(zblock, dtype=jnp.int32)[None, :]).reshape(-1, 1)
    fine = jnp.arange(nz, dtype=jnp.int32)[None, :]
    weights = jnp.where(fine == 2 * target, 0.5, 0.0) + jnp.where(
        (fine == 2 * target + 1) | (fine == 2 * target - 1), 0.25, 0.0
    )

    square = ((LANES, LANES), f32)
    half = ((levels * zblock, LANES), f32)
    edge_rows = (FIELDS * OUTER + 2, LANES)
    smoothed, own, to_a, to_b = call(
        last_kernel, [whole, half, half, half],
        [whole[0], strip, strip, strip, strip, corner, (FIELDS * OUTER * SIDE, LANES),
         edge_rows, edge_rows, edge_rows, edge_rows, (3 * LANES, LANES)],
        cells, *params, f_got, n_got, b_got, a_got, *old, weights.astype(bf16),
    )
    smoothed = smoothed.reshape(adjoint.shape)
    a_got = lax.all_gather(to_a, "brick", axis_index_groups=a_groups)
    (send,) = call(send_kernel, [square], [], own, a_got, to_b)
    send = send.reshape(2 * levels, zblock, LANES)
    got = lax.all_to_all(
        send, BOTH, split_axis=0, concat_axis=0, tiled=True, axis_index_groups=columns
    )
    (coarse_rhs,) = call(
        functools.partial(final_kernel, bricks), [((FIELDS * HALF * zblock, levels * HALF), f32)],
        [square[0]], got.reshape(LANES, LANES),
    )
    coarse_rhs = coarse_rhs.reshape(FIELDS, HALF, zblock, levels * HALF)
    coarse_rhs = coarse_rhs.transpose(0, 3, 1, 2)[None]
    return (smoothed, coarse_rhs)


def solution(mesh):
    placed = (
        P(None, "level", "brick", None),
        P(None, "level", "brick", None),
        P(None, None, "level", "brick", None),
        P(None, None, "level", "brick", None),
        P(None, "level", "brick", None),
        P("level", "brick", None),
        P(),
    )
    return jax.shard_map(
        shards,
        mesh=mesh,
        in_specs=placed,
        out_specs=(P(None, "level", "brick", None), P("level", None, None, "brick", None)),
        check_vma=False,
    )
```
